256 devices in a mesh: gx: 32 (over z_hi, x, core), gy: 4 (over y), row: 2 (over z_lo).
Axes of the slice: x: 4, y: 4, z: 8 (z_hi: 4, z_lo: 2; z = z_hi * 2 + z_lo), core: 2. Of those that a mesh axis runs over, the one named last changes fastest.
Arguments:
- concentrations: float32 [2, 512, 128, 256], P(None, 'gx', 'gy', 'row'), may hold values from 0 to 1
- diffusivity: float32 [512, 128, 256], P('gx', 'gy', 'row'), may hold values from 0.25 to 1
- weight_first: bfloat16 [512, 1024], replicated, may hold values from -0.25 to 0.25
- weight_middle: bfloat16 [1024, 1024], replicated, may hold values from -0.1875 to 0.1875
- weight_last: bfloat16 [1024, 512], replicated, may hold values from -0.1875 to 0.1875
Outputs:
- concentrations_out: float32 [2, 512, 128, 256], P(None, 'gx', 'gy', 'row')
- grad_first: float32 [512, 1024], P(('gx', 'gy', 'row'))
- grad_middle: float32 [1024, 1024], P(('gx', 'gy', 'row'))
- grad_last: float32 [1024, 512], P(('gx', 'gy', 'row'))
The draws below stay inside these ranges and needn't reach their ends.
All inputs are finite; a program needn't handle non-finite values.
Results may differ from the reference program's by a relative error of at most 0.00035.
Values may be sent and summed in bfloat16 or wider, within the bound.
A program may use at most 128 MiB of HBM per device.

```python
import math
import jax
import jax.numpy as jnp
from jax import lax

STEPS = 6
PATCH = 8
HID = 1024
CELLS = 512
PATCHES_DEV = 128
NX = 512
NY = 128
NZ = 256


def steps_of(key, extent, split, least, largest):
    level, own = 1.0, jax.random.fold_in(key, 6)
    for position, parts in split:
        steps = jnp.exp(jax.random.uniform(jax.random.fold_in(own, position), (parts,), jnp.float32, least / len(split), largest / len(split)))
        level = level * jnp.repeat(steps, extent[position] // parts).reshape([-1 if axis == position else 1 for axis in range(len(extent))])
    return level


def gaussian(own_key, extent, spread, most, held_as=jnp.bfloat16):
    array = jax.random.normal(own_key, extent, jnp.float32) * spread
    return jnp.minimum(jnp.maximum(array, -most), most).astype(held_as)


def setup_inputs(seed: int = 0) -> dict:
    seeds = jax.random.split(jax.random.key(seed), 6)
    concentrations = jnp.clip(1.0 * jax.random.uniform(seeds[0], (2, NX, NY, NZ), jnp.float32) ** steps_of(seeds[0], (2, NX, NY, NZ), ((1, 32), (2, 4), (3, 2)), -0.2, 0.2), 0.0, 1.0)
    diffusivity = jnp.clip(jnp.exp(math.log(1.0) - 1.3862944 * jax.random.uniform(seeds[1], (NX, NY, NZ), jnp.float32) ** steps_of(seeds[1], (NX, NY, NZ), ((0, 32), (1, 4), (2, 2)), -0.2, 0.2)), 0.25, 1.0)
    weight_first = gaussian(seeds[2], (CELLS, HID), CELLS ** -0.5, 0.25)
    weight_middle = gaussian(seeds[3], (HID, HID), HID ** -0.5, 0.1875)
    weight_last = gaussian(seeds[4], (HID, CELLS), HID ** -0.5, 0.1875)
    return dict(concentrations=concentrations, diffusivity=diffusivity, weight_first=weight_first, weight_middle=weight_middle, weight_last=weight_last)


def laplace(values):
    summed = -6.0 * values
    for dimension in range(3):
        summed = summed + jnp.roll(values, 1, dimension) + jnp.roll(values, -1, dimension)
    return summed

def react(activator, inhibitor, diffusivity, lap_activator, lap_inhibitor, forcing):
    product = activator * inhibitor * inhibitor
    new_activator = activator + 0.1 * (diffusivity * lap_activator - product + 0.04 * (1.0 - activator) + forcing)
    new_inhibitor = inhibitor + 0.1 * (0.5 * diffusivity * lap_inhibitor + product - 0.1 * inhibitor)
    return (new_activator, new_inhibitor)

def to_patches(values, edge):
    extent_x, extent_y, extent_z = values.shape
    pieces = values.reshape(extent_x // edge, edge, extent_y // edge, edge, extent_z // edge, edge)
    return pieces.transpose(0, 2, 4, 1, 3, 5).reshape(-1, edge * edge * edge)

def from_patches(rows, shape, edge):
    extent_x, extent_y, extent_z = shape
    pieces = rows.reshape(extent_x // edge, extent_y // edge, extent_z // edge, edge, edge, edge)
    return pieces.transpose(0, 3, 1, 4, 2, 5).reshape(extent_x, extent_y, extent_z)

def gelu_back(pre_values, cotangent):
    unused, puller = jax.vjp(jax.nn.gelu, pre_values)
    return puller(cotangent)[0]

def learner(inputs, targets, weight_first, weight_middle, weight_last, scale):
    contract_rows = (((0,), (0,)), ((), ()))
    contract_cols = (((1,), (1,)), ((), ()))
    pre_first = jnp.dot(inputs, weight_first, preferred_element_type=jnp.float32)
    hidden_first = jax.nn.gelu(pre_first).astype(jnp.bfloat16)
    pre_second = jnp.dot(hidden_first, weight_middle, preferred_element_type=jnp.float32)
    hidden_second = jax.nn.gelu(pre_second).astype(jnp.bfloat16)
    forcing = jnp.dot(hidden_second, weight_last, preferred_element_type=jnp.float32)
    error = ((forcing - targets.astype(jnp.float32)) * scale).astype(jnp.bfloat16)
    grad_last = lax.dot_general(hidden_second, error, contract_rows, preferred_element_type=jnp.float32)
    carried = lax.dot_general(error, weight_last, contract_cols, preferred_element_type=jnp.float32)
    back_second = gelu_back(pre_second, carried).astype(jnp.bfloat16)
    grad_middle = lax.dot_general(hidden_first, back_second, contract_rows, preferred_element_type=jnp.float32)
    carried = lax.dot_general(back_second, weight_middle, contract_cols, preferred_element_type=jnp.float32)
    back_first = gelu_back(pre_first, carried).astype(jnp.bfloat16)
    grad_first = lax.dot_general(inputs, back_first, contract_rows, preferred_element_type=jnp.float32)
    return (forcing, grad_first, grad_middle, grad_last)

def reference(concentrations, diffusivity, weight_first, weight_middle, weight_last):
    activator = concentrations[0]
    inhibitor = concentrations[1]
    zero_force = jnp.zeros_like(activator)
    for repeat in range(STEPS // 2):
        activator, inhibitor = react(activator, inhibitor, diffusivity, laplace(activator), laplace(inhibitor), zero_force)
    inputs = to_patches(activator, PATCH).astype(jnp.bfloat16).reshape(-1, PATCHES_DEV, CELLS)
    targets = to_patches(inhibitor, PATCH).astype(jnp.bfloat16).reshape(-1, PATCHES_DEV, CELLS)
    scale = 1.0 / PATCHES_DEV

    def one_block(carry, block):
        forcing, grad_first, grad_middle, grad_last = learner(block[0], block[1], weight_first, weight_middle, weight_last, scale)
        return ((carry[0] + grad_first, carry[1] + grad_middle, carry[2] + grad_last), forcing)
    start = (jnp.zeros(weight_first.shape, jnp.float32), jnp.zeros(weight_middle.shape, jnp.float32), jnp.zeros(weight_last.shape, jnp.float32))
    grads, forcing_rows = lax.scan(one_block, start, (inputs, targets))
    forcing_field = from_patches(forcing_rows.reshape(-1, CELLS), activator.shape, PATCH)
    for repeat in range(STEPS - STEPS // 2):
        activator, inhibitor = react(activator, inhibitor, diffusivity, laplace(activator), laplace(inhibitor), forcing_field)
    return (jnp.stack([activator, inhibitor]), grads[0], grads[1], grads[2])
```

```python
import jax
import jax.numpy as jnp
from jax import lax
from jax.experimental import pallas as pl
from jax.experimental.pallas import tpu as pltpu
from jax.sharding import PartitionSpec as P

STEPS = 6
F32 = jnp.float32
BF16 = jnp.bfloat16
MESH = pl.DeviceIdType.MESH
BLOCKS = 8
GELU_A = 0.7978845608028654
GELU_B = 0.044715


def place():
    gx, gy, row = lax.axis_index("gx"), lax.axis_index("gy"), lax.axis_index("row")
    return {"core": gx % 2, "x": (gx // 2) % 4, "y": gy, "z": (gx // 8) * 2 + row}


def device(at):
    return {
        "gx": (at["z"] // 2) * 8 + at["x"] * 2 + at["core"],
        "gy": at["y"],
        "row": at["z"] % 2,
    }


def moved(at, axis, distance):
    size = {"core": 2, "x": 4, "y": 4, "z": 8}[axis]
    return device({**at, axis: (at[axis] + distance) % size})


def gelu_pair(values):
    squared = values * values
    bent = jnp.tanh(GELU_A * (values + GELU_B * (values * squared)))
    half = 0.5 * (1.0 + bent)
    slope = half + (0.5 * values) * (1.0 - bent * bent) * (
        GELU_A + (3.0 * GELU_A * GELU_B) * squared
    )
    return values * half, slope


def rows_of(left, right):
    return lax.dot_general(left, right, (((1,), (0,)), ((), ())), preferred_element_type=F32)


def rows_of_t(left, right):
    return lax.dot_general(left, right, (((1,), (1,)), ((), ())), preferred_element_type=F32)


def kernel(
    conc, diff_in, wf_in, wm_in, wl_in,
    conc_out, gf_out, gm_out, gl_out,
    st, diff, ysend, zsend, hy, hz, tiles_u, tiles_v, turned, forced,
    wf, wm, wl, order, primed, inputs, targets, slope1, slope2, hidden,
    left, left_in, right, grad, recv1, sum1, recv2, pack, recv3, fin,
    load_sem, out_sem, halo_send, halo_recv, pair_send, pair_recv,
    send1, take1, send2, take2, send3, take3,
):
    at = place()
    gx, gy, row = lax.axis_index("gx"), lax.axis_index("gy"), lax.axis_index("row")
    mate = moved(at, "core", 1)
    core = at["core"]

    loads = [
        pltpu.make_async_copy(conc, st.at[0, :, pl.ds(1, 16)], load_sem.at[0]),
        pltpu.make_async_copy(diff_in, diff, load_sem.at[1]),
        pltpu.make_async_copy(wf_in, wf, load_sem.at[2]),
        pltpu.make_async_copy(wm_in, wm, load_sem.at[3]),
        pltpu.make_async_copy(wl_in, wl, load_sem.at[4]),
    ]
    for copy in loads:
        copy.start()

    barrier = pltpu.get_barrier_semaphore()
    peers = [{"gx": (gx + 1) % 32}, {"gx": (gx + 31) % 32}]
    peers += [moved(at, "x", d) for d in (1, 2, 3)]
    peers += [moved(at, "y", d) for d in (1, 2, 3)]
    peers += [moved(at, "z", d) for d in range(1, 8)]
    for peer in peers:
        pl.semaphore_signal(barrier, inc=1, device_id=peer, device_id_type=MESH)

    iota_y = lax.broadcasted_iota(jnp.int32, (32, 128), 0)
    iota_z = lax.broadcasted_iota(jnp.int32, (32, 128), 1)

    def face_rows(par, x, new, packed):
        for f in (0, 1):
            ysend[par, 0, f, pl.ds(x, 1), :] = new[f][0:1, :]
            ysend[par, 1, f, pl.ds(x, 1), :] = new[f][31:32, :]
            k = f * 16 + x
            packed = jnp.where(iota_z == k, pltpu.roll(new[f], k, 1), packed)
            packed = jnp.where(iota_z == k + 32, pltpu.roll(new[f], k + 33, 1), packed)
        return packed

    def halo_copies(par):
        plan = [
            (st.at[par, :, 1], st.at[par, :, 17], {"gx": (gx + 31) % 32}),
            (st.at[par, :, 16], st.at[par, :, 0], {"gx": (gx + 1) % 32}),
            (ysend.at[par, 0], hy.at[par, 1], {"gy": (gy + 3) % 4}),
            (ysend.at[par, 1], hy.at[par, 0], {"gy": (gy + 1) % 4}),
            (zsend.at[par], hz.at[par], {"row": 1 - row}),
        ]
        return [
            pltpu.make_async_remote_copy(
                src_ref=src, dst_ref=dst,
                send_sem=halo_send.at[par, i], recv_sem=halo_recv.at[par, i],
                device_id=who, device_id_type=MESH,
            )
            for i, (src, dst, who) in enumerate(plan)
        ]

    def step(number, force):
        par, nxt = number % 2, (number + 1) % 2
        for copy in halo_copies(par):
            copy.wait_recv()
        if number >= 1:
            for copy in halo_copies(nxt):
                copy.wait_send()
        last = number == STEPS - 1

        def body(x, packed):
            hzv = hz[par]
            laps, centers = [], []
            for f in (0, 1):
                c = st[par, f, x + 1]
                y_next = hy[par, 1, f, pl.ds(x, 1), :]
                y_prev = hy[par, 0, f, pl.ds(x, 1), :]
                k = f * 16 + x
                yp = jnp.where(iota_y == 31, y_next, pltpu.roll(c, 31, 0))
                ym = jnp.where(iota_y == 0, y_prev, pltpu.roll(c, 1, 0))
                zp = jnp.where(iota_z == 127, pltpu.roll(hzv, 127 - k, 1), pltpu.roll(c, 127, 1))
                zm = jnp.where(iota_z == 0, pltpu.roll(hzv, 96 - k, 1), pltpu.roll(c, 1, 1))
                lap = -6.0 * c + st[par, f, x + 2] + st[par, f, x] + yp + ym + zp + zm
                laps.append(lap)
                centers.append(c)
            u, v = centers
            d = diff[x]
            product = u * v * v
            inner = d * laps[0] - product + 0.04 * (1.0 - u)
            if force:
                base = (x // 8) * 256 + (x % 8) * 8
                inner = inner + jnp.concatenate(
                    [forced[pl.ds(pl.multiple_of(base + py * 64, 8), 8), :] for py in range(4)], axis=0
                )
            new_u = u + 0.1 * inner
            new_v = v + 0.1 * (0.5 * d * laps[1] + product - 0.1 * v)
            st[nxt, 0, x + 1] = new_u
            st[nxt, 1, x + 1] = new_v
            if number == STEPS // 2 - 1:
                base = (x // 8) * 256 + (x % 8) * 8
                for py in range(4):
                    here = pl.ds(pl.multiple_of(base + py * 64, 8), 8)
                    tiles_u[here, :] = new_u[py * 8:py * 8 + 8, :]
                    tiles_v[here, :] = new_v[py * 8:py * 8 + 8, :]
            if last:
                return packed
            return face_rows(nxt, x, (new_u, new_v), packed)

        packed = lax.fori_loop(0, 16, body, jnp.zeros((32, 128), F32))
        if not last:
            zsend[nxt] = packed
            for copy in halo_copies(nxt):
                copy.start()

    loads[0].wait()

    def first_faces(x, packed):
        return face_rows(0, x, (st[0, 0, x + 1], st[0, 1, x + 1]), packed)

    zsend[0] = lax.fori_loop(0, 16, first_faces, jnp.zeros((32, 128), F32))
    pl.semaphore_wait(barrier, len(peers))
    for copy in halo_copies(0):
        copy.start()

    r = lax.broadcasted_iota(jnp.int32, (512, 512), 0)
    c = lax.broadcasted_iota(jnp.int32, (512, 512), 1)
    order[0] = jnp.where(c == (r % 64) * 8 + r // 64, 1.0, 0.0).astype(BF16)
    for half in (0, 1):
        cell = (r // 128) * 128 + ((r // 32) % 4) * 32 + half * 16
        cell = cell + ((r // 8) % 4) * 4 + ((r // 4) % 2) * 2 + r % 2
        order[1 + half] = jnp.where(c == cell, 1.0, 0.0).astype(BF16)

    loads[1].wait()
    step(0, False)
    step(1, False)
    step(2, False)

    low = lax.broadcasted_iota(jnp.int32, (16, 128), 1) < 64
    for tiles, result in ((tiles_u, inputs), (tiles_v, targets)):
        for q in range(4):
            turned[q] = tiles[q * 128:q * 128 + 128, :].T
        for m in range(4):
            for q in range(4):
                a = turned[q, pl.ds(2 * m, 16, stride=8), :]
                b = turned[q, pl.ds(2 * m + 1, 16, stride=8), :]
                even = jnp.where(low, a, pltpu.roll(b, 64, 1))
                odd = jnp.where(low, pltpu.roll(a, 64, 1), b)
                primed[q * 32:q * 32 + 16, m * 128:m * 128 + 128] = even.astype(BF16)
                primed[q * 32 + 16:q * 32 + 32, m * 128:m * 128 + 128] = odd.astype(BF16)
        result[...] = rows_of(primed[...], order[0]).astype(BF16)

    def pair_copy(i):
        if i < 3:
            src = left_in.at[1 - core] if i == 0 else left.at[i - 1, 1 - core]
            dst = left_in.at[2] if i == 0 else left.at[i - 1, 2]
        else:
            cols = pl.ds(*((0, 1024), (1024, 1024), (2048, 512))[i - 3])
            src, dst = right.at[0, :, cols], right.at[1, :, cols]
        return pltpu.make_async_remote_copy(
            src_ref=src, dst_ref=dst, send_sem=pair_send.at[i], recv_sem=pair_recv.at[i],
            device_id=mate, device_id_type=MESH,
        )

    def layer(source, weights, slopes, which):
        def body(j, carry):
            cols = pl.ds(pl.multiple_of(j * 256, 256), 256)
            value, slope = gelu_pair(rows_of(source[...], weights[:, cols]))
            slopes[:, cols] = slope
            hidden[which, :, cols] = value.astype(BF16)
            flipped = value.T.astype(BF16)
            for x in range(4):
                for half in (0, 1):
                    left[which, half, pl.ds(pl.multiple_of((j * 4 + x) * 32, 32), 32), :] = flipped[
                        x * 64 + half * 32:x * 64 + half * 32 + 32, :
                    ]
            return carry

        lax.fori_loop(0, 4, body, 0)

    loads[2].wait()
    layer(inputs, wf, slope1, 0)
    pair_copy(1).start()
    for half in (0, 1):
        left_in[half] = rows_of_t(order[1 + half], inputs[...]).astype(BF16)
    pair_copy(0).start()
    loads[3].wait()
    layer(hidden.at[0], wm, slope2, 1)
    pair_copy(2).start()
    loads[4].wait()
    forcing = rows_of(hidden[1], wl[...])
    right[0, :, 2048:2560] = ((forcing - targets[...].astype(F32)) * (1.0 / 128)).astype(BF16)
    pair_copy(5).start()

    top = forcing.astype(BF16)
    rest = forcing - top.astype(F32)
    middle = rest.astype(BF16)
    rest = (rest - middle.astype(F32)).astype(BF16)
    back = rows_of_t(top, order[0]) + rows_of_t(middle, order[0]) + rows_of_t(rest, order[0])
    for m in range(4):
        for q in range(4):
            even = back[q * 32:q * 32 + 16, m * 128:m * 128 + 128]
            odd = back[q * 32 + 16:q * 32 + 32, m * 128:m * 128 + 128]
            turned[q, pl.ds(2 * m, 16, stride=8), :] = jnp.where(low, even, pltpu.roll(odd, 64, 1))
            turned[q, pl.ds(2 * m + 1, 16, stride=8), :] = jnp.where(low, pltpu.roll(even, 64, 1), odd)
    for q in range(4):
        forced[q * 128:q * 128 + 128, :] = turned[q].T
    step(3, True)

    def backward(error_cols, weights, slopes, first_col):
        def body(j, carry):
            cols = pl.ds(pl.multiple_of(j * 256, 256), 256)
            carried = rows_of_t(right[0, :, error_cols], weights[cols, :])
            right[0, :, pl.ds(pl.multiple_of(first_col + j * 256, 256), 256)] = (
                carried * slopes[:, cols]
            ).astype(BF16)
            return carry

        lax.fori_loop(0, 4, body, 0)

    def stage(b, number, d):
        axis = "xy"[(b + number) % 2]
        if number == 0:
            src, dst, send, take = grad.at[b], recv1.at[b, d - 1], send1, take1
        else:
            src, dst, send, take = sum1.at[b], recv2.at[b, d - 1], send2, take2
        return pltpu.make_async_remote_copy(
            src_ref=src.at[(at[axis] + d) % 4], dst_ref=dst,
            send_sem=send.at[b, d - 1], recv_sem=take.at[b, d - 1],
            device_id=moved(at, axis, d), device_id_type=MESH,
        )

    def gradient(b, own, other, cols):
        both = jnp.concatenate([own, other], axis=1)
        columns = jnp.concatenate([right[0, :, cols], right[1, :, cols]], axis=0)
        return rows_of(both, columns)

    def keep(b, value):
        cut = value.reshape(4, 4, 4, 8, 256)
        for i in range(4):
            grad[b, i] = cut[:, i] if b % 2 == 0 else cut[:, :, i]
        for d in (1, 2, 3):
            stage(b, 0, d).start()

    backward(pl.ds(2048, 512), wl, slope2, 1024)
    pair_copy(4).start()
    pair_copy(2).wait_recv()
    pair_copy(5).wait_recv()
    for b in (0, 1):
        keep(b, gradient(b, left[1, core], left[1, 2], slice(2048 + b * 256, 2304 + b * 256)))
    backward(pl.ds(1024, 1024), wm, slope1, 0)
    pair_copy(3).start()
    pair_copy(1).wait_recv()
    pair_copy(4).wait_recv()
    for b in (2, 3, 4, 5):
        col = 1024 + (b - 2) * 256
        keep(b, gradient(b, left[0, core], left[0, 2], slice(col, col + 256)))
    pair_copy(0).wait_recv()
    pair_copy(3).wait_recv()
    upper = (lax.broadcasted_iota(jnp.int32, (512, 256), 0) // 2) % 2 == 0
    for b in (6, 7):
        col = (b - 6) * 256
        keep(
            b,
            jnp.where(
                upper,
                gradient(b, left_in[core], left_in[2], slice(col, col + 256)),
                gradient(b, left_in[core], left_in[2], slice(col + 512, col + 768)),
            ),
        )

    step(4, True)

    sub = lax.broadcasted_iota(jnp.int32, (8, 128), 0) < 4

    def after_first(b):
        axis = "xy"[b % 2]
        for d in (1, 2, 3):
            stage(b, 0, d).wait_recv()
        total = grad[b, at[axis]] + recv1[b, 0] + recv1[b, 1] + recv1[b, 2]
        for i in range(4):
            sum1[b, i] = total[:, i]
        for d in (1, 2, 3):
            stage(b, 1, d).start()

    def after_second(b):
        axis = "xy"[(b + 1) % 2]
        for d in (1, 2, 3):
            stage(b, 1, d).wait_recv()
        total = sum1[b, at[axis]] + recv2[b, 0] + recv2[b, 1] + recv2[b, 2]
        for zh in range(4):
            lo, hi = total[zh, :, :128], total[zh, :, 128:]
            here = slice(b * 128, b * 128 + 128)
            pack[2 * zh, :, here] = jnp.where(sub, lo, pltpu.roll(hi, 4, 0))
            pack[2 * zh + 1, :, here] = jnp.where(sub, pltpu.roll(lo, 4, 0), hi)

    def stage3(d):
        return pltpu.make_async_remote_copy(
            src_ref=pack.at[(at["z"] + d) % 8], dst_ref=recv3.at[d - 1],
            send_sem=send3.at[d - 1], recv_sem=take3.at[d - 1],
            device_id=moved(at, "z", d), device_id_type=MESH,
        )

    for b in range(BLOCKS):
        after_first(b)
    step(5, True)
    out = pltpu.make_async_copy(st.at[0, :, pl.ds(1, 16)], conc_out, out_sem)
    out.start()
    for b in range(BLOCKS):
        after_second(b)
    for d in range(1, 8):
        stage3(d).start()
    for d in range(1, 8):
        stage3(d).wait_recv()
    total = pack[at["z"]]
    for d in range(7):
        total = total + recv3[d]

    def wide(b):
        part = total[:, b * 128:b * 128 + 128]
        return jnp.concatenate([part[0:4], part[4:8]], axis=1)

    gl_out[...] = jnp.concatenate([wide(0), wide(1)], axis=1)
    gm_out[...] = jnp.concatenate([wide(b) for b in (2, 3, 4, 5)], axis=1)
    whole = jnp.concatenate([wide(6), wide(7)], axis=1)
    gf_out[...] = jnp.concatenate([whole[0:2], whole[2:4]], axis=1)

    out.wait()
    for i in range(6):
        pair_copy(i).wait_send()
    for b in range(BLOCKS):
        for d in (1, 2, 3):
            stage(b, 0, d).wait_send()
            stage(b, 1, d).wait_send()
    for d in range(1, 8):
        stage3(d).wait_send()
    for copy in halo_copies((STEPS - 1) % 2):
        copy.wait_send()


def per_device(concentrations, diffusivity, weight_first, weight_middle, weight_last):
    any_space = pl.BlockSpec(memory_space=pl.ANY)
    vmem = pl.BlockSpec(memory_space=pltpu.VMEM)
    dma = pltpu.SemaphoreType.DMA
    return pl.pallas_call(
        kernel,
        out_shape=(
            jax.ShapeDtypeStruct((2, 16, 32, 128), F32),
            jax.ShapeDtypeStruct((2, 1024), F32),
            jax.ShapeDtypeStruct((4, 1024), F32),
            jax.ShapeDtypeStruct((4, 512), F32),
        ),
        in_specs=[any_space] * 5,
        out_specs=(any_space, vmem, vmem, vmem),
        scratch_shapes=[
            pltpu.VMEM((2, 2, 18, 32, 128), F32),
            pltpu.VMEM((16, 32, 128), F32),
            pltpu.VMEM((2, 2, 2, 16, 128), F32),
            pltpu.VMEM((2, 32, 128), F32),
            pltpu.VMEM((2, 2, 2, 16, 128), F32),
            pltpu.VMEM((2, 32, 128), F32),
            pltpu.VMEM((512, 128), F32),
            pltpu.VMEM((512, 128), F32),
            pltpu.VMEM((4, 128, 128), F32),
            pltpu.VMEM((512, 128), F32),
            pltpu.VMEM((512, 1024), BF16),
            pltpu.VMEM((1024, 1024), BF16),
            pltpu.VMEM((1024, 512), BF16),
            pltpu.VMEM((3, 512, 512), BF16),
            pltpu.VMEM((128, 512), BF16),
            pltpu.VMEM((128, 512), BF16),
            pltpu.VMEM((128, 512), BF16),
            pltpu.VMEM((128, 1024), F32),
            pltpu.VMEM((128, 1024), F32),
            pltpu.VMEM((2, 128, 1024), BF16),
            pltpu.VMEM((2, 3, 512, 128), BF16),
            pltpu.VMEM((3, 512, 128), BF16),
            pltpu.VMEM((2, 128, 2560), BF16),
            pltpu.VMEM((BLOCKS, 4, 4, 4, 8, 256), F32),
            pltpu.VMEM((BLOCKS, 3, 4, 4, 8, 256), F32),
            pltpu.VMEM((BLOCKS, 4, 4, 8, 256), F32),
            pltpu.VMEM((BLOCKS, 3, 4, 8, 256), F32),
            pltpu.VMEM((8, 8, BLOCKS * 128), F32),
            pltpu.VMEM((7, 8, BLOCKS * 128), F32),
            pltpu.VMEM((8, BLOCKS * 128), F32),
            dma((5,)), dma, dma((2, 5)), dma((2, 5)), dma((6,)), dma((6,)),
            dma((BLOCKS, 3)), dma((BLOCKS, 3)), dma((BLOCKS, 3)), dma((BLOCKS, 3)),
            dma((7,)), dma((7,)),
        ],
        compiler_params=pltpu.CompilerParams(
            collective_id=0, has_side_effects=True, vmem_limit_bytes=56 << 20
        ),
        name="whole_step",
    )(concentrations, diffusivity, weight_first, weight_middle, weight_last)


def solution(mesh):
    in_specs = (P(None, "gx", "gy", "row"), P("gx", "gy", "row"), P(), P(), P())
    out_specs = (
        P(None, "gx", "gy", "row"),
        P(("gx", "gy", "row"), None),
        P(("gx", "gy", "row"), None),
        P(("gx", "gy", "row"), None),
    )
    return jax.shard_map(
        per_device, mesh=mesh, in_specs=in_specs, out_specs=out_specs, check_vma=False
    )
```

```python
import jax
import jax.numpy as jnp
from jax import lax
from jax.experimental import pallas as pl
from jax.experimental.pallas import tpu as pltpu
from jax.sharding import PartitionSpec as P

STEPS = 6
F32 = jnp.float32
BF16 = jnp.bfloat16
MESH = pl.DeviceIdType.MESH
BLOCKS = 8
GELU_A = 0.7978845608028654
GELU_B = 0.044715


def place():
    gx, gy, row = lax.axis_index("gx"), lax.axis_index("gy"), lax.axis_index("row")
    return {"core": gx % 2, "x": (gx // 2) % 4, "y": gy, "z": (gx // 8) * 2 + row}


def device(at):
    return {
        "gx": (at["z"] // 2) * 8 + at["x"] * 2 + at["core"],
        "gy": at["y"],
        "row": at["z"] % 2,
    }


def moved(at, axis, distance):
    size = {"core": 2, "x": 4, "y": 4, "z": 8}[axis]
    return device({**at, axis: (at[axis] + distance) % size})


def gelu_pair(values):
    squared = values * values
    bent = jnp.tanh(GELU_A * (values + GELU_B * (values * squared)))
    half = 0.5 * (1.0 + bent)
    slope = half + (0.5 * values) * (1.0 - bent * bent) * (
        GELU_A + (3.0 * GELU_A * GELU_B) * squared
    )
    return values * half, slope


def rows_of(left, right):
    return lax.dot_general(left, right, (((1,), (0,)), ((), ())), preferred_element_type=F32)


def rows_of_t(left, right):
    return lax.dot_general(left, right, (((1,), (1,)), ((), ())), preferred_element_type=F32)


def kernel(
    conc, diff_in, wf_in, wm_in, wl_in,
    conc_out, sums_out,
    st, diff, ysend, zsend, hy, hz, tiles_u, tiles_v, turned, forced,
    wf, wm, wl, order, primed, inputs, targets, slope1, slope2, hidden,
    left, left_in, right, grad, recv1, sum1, recv2, pack, recv3,
    load_sem, out_sem, halo_send, halo_recv, pair_send, pair_recv,
    send1, take1, send2, take2, send3, take3,
):
    at = place()
    gx, gy, row = lax.axis_index("gx"), lax.axis_index("gy"), lax.axis_index("row")
    mate = moved(at, "core", 1)
    core = at["core"]

    loads = [
        pltpu.make_async_copy(conc, st.at[0, :, pl.ds(1, 16)], load_sem.at[0]),
        pltpu.make_async_copy(diff_in, diff, load_sem.at[1]),
        pltpu.make_async_copy(wf_in, wf, load_sem.at[2]),
        pltpu.make_async_copy(wm_in, wm, load_sem.at[3]),
        pltpu.make_async_copy(wl_in, wl, load_sem.at[4]),
    ]
    for copy in loads:
        copy.start()

    barrier = pltpu.get_barrier_semaphore()
    peers = [{"gx": (gx + 1) % 32}, {"gx": (gx + 31) % 32}]
    peers += [moved(at, "x", d) for d in (1, 2, 3)]
    peers += [moved(at, "y", d) for d in (1, 2, 3)]
    peers += [moved(at, "z", d) for d in range(1, 8)]
    for peer in peers:
        pl.semaphore_signal(barrier, inc=1, device_id=peer, device_id_type=MESH)

    iota_y = lax.broadcasted_iota(jnp.int32, (32, 128), 0)
    iota_z = lax.broadcasted_iota(jnp.int32, (32, 128), 1)
    pair_z = iota_z // 2

    def face_rows(par, x, new, packed):
        for f in (0, 1):
            ysend[par, 0, f, pl.ds(x, 1), :] = new[f][0:1, :]
            ysend[par, 1, f, pl.ds(x, 1), :] = new[f][31:32, :]
            k = f * 16 + x
            packed = jnp.where(pair_z == k, pltpu.roll(new[f], 2 * k + 1, 1), packed)
        return packed

    def halo_copies(par):
        plan = [
            (st.at[par, :, 1], st.at[par, :, 17], {"gx": (gx + 31) % 32}),
            (st.at[par, :, 16], st.at[par, :, 0], {"gx": (gx + 1) % 32}),
            (ysend.at[par, 0], hy.at[par, 1], {"gy": (gy + 3) % 4}),
            (ysend.at[par, 1], hy.at[par, 0], {"gy": (gy + 1) % 4}),
            (zsend.at[par], hz.at[par], {"row": 1 - row}),
        ]
        return [
            pltpu.make_async_remote_copy(
                src_ref=src, dst_ref=dst,
                send_sem=halo_send.at[par, i], recv_sem=halo_recv.at[par, i],
                device_id=who, device_id_type=MESH,
            )
            for i, (src, dst, who) in enumerate(plan)
        ]

    def step(number, force):
        par, nxt = number % 2, (number + 1) % 2
        for copy in halo_copies(par)[2:]:
            copy.wait_recv()
        if number >= 1:
            for copy in halo_copies(nxt):
                copy.wait_send()
        last = number == STEPS - 1

        def body(x, packed):
            hzv = hz[par]
            laps, centers = [], []
            for f in (0, 1):
                c = st[par, f, x + 1]
                y_next = hy[par, 1, f, pl.ds(x, 1), :]
                y_prev = hy[par, 0, f, pl.ds(x, 1), :]
                k = f * 16 + x
                yp = jnp.where(iota_y == 31, y_next, pltpu.roll(c, 31, 0))
                ym = jnp.where(iota_y == 0, y_prev, pltpu.roll(c, 1, 0))
                edges = pltpu.roll(hzv, 127 - 2 * k, 1)
                zp = pltpu.roll(jnp.where(iota_z == 0, edges, c), 127, 1)
                zm = pltpu.roll(jnp.where(iota_z == 127, edges, c), 1, 1)
                lap = -6.0 * c + st[par, f, x + 2] + st[par, f, x] + yp + ym + zp + zm
                laps.append(lap)
                centers.append(c)
            u, v = centers
            d = diff[x]
            product = u * v * v
            inner = d * laps[0] - product + 0.04 * (1.0 - u)
            if force:
                base = (x // 8) * 256 + (x % 8) * 8
                inner = inner + jnp.concatenate(
                    [forced[pl.ds(pl.multiple_of(base + py * 64, 8), 8), :] for py in range(4)], axis=0
                )
            new_u = u + 0.1 * inner
            new_v = v + 0.1 * (0.5 * d * laps[1] + product - 0.1 * v)
            st[nxt, 0, x + 1] = new_u
            st[nxt, 1, x + 1] = new_v
            if number == STEPS // 2 - 1:
                base = (x // 8) * 256 + (x % 8) * 8
                for py in range(4):
                    here = pl.ds(pl.multiple_of(base + py * 64, 8), 8)
                    tiles_u[here, :] = new_u[py * 8:py * 8 + 8, :]
                    tiles_v[here, :] = new_v[py * 8:py * 8 + 8, :]
            if last:
                return packed
            return face_rows(nxt, x, (new_u, new_v), packed)

        packed = lax.fori_loop(2, 14, body, jnp.zeros((32, 128), F32), unroll=4)
        for copy in halo_copies(par)[:2]:
            copy.wait_recv()
        for x in (0, 1, 14, 15):
            packed = body(x, packed)
        if not last:
            zsend[nxt] = packed
            for copy in halo_copies(nxt):
                copy.start()

    loads[0].wait()

    def first_faces(x, packed):
        return face_rows(0, x, (st[0, 0, x + 1], st[0, 1, x + 1]), packed)

    zsend[0] = lax.fori_loop(0, 16, first_faces, jnp.zeros((32, 128), F32), unroll=4)
    pl.semaphore_wait(barrier, len(peers))
    for copy in halo_copies(0):
        copy.start()

    r = lax.broadcasted_iota(jnp.int32, (512, 512), 0)
    c = lax.broadcasted_iota(jnp.int32, (512, 512), 1)
    order[0] = jnp.where(c == (r % 64) * 8 + r // 64, 1.0, 0.0).astype(BF16)
    for half in (0, 1):
        cell = (r // 128) * 128 + ((r // 32) % 4) * 32 + half * 16
        cell = cell + ((r // 8) % 4) * 4 + ((r // 4) % 2) * 2 + r % 2
        order[1 + half] = jnp.where(c == cell, 1.0, 0.0).astype(BF16)

    loads[1].wait()
    step(0, False)
    step(1, False)
    step(2, False)

    low = lax.broadcasted_iota(jnp.int32, (16, 128), 1) < 64
    for tiles, result in ((tiles_u, inputs), (tiles_v, targets)):
        for q in range(4):
            turned[q] = tiles[q * 128:q * 128 + 128, :].T
        for m in range(4):
            for q in range(4):
                a = turned[q, pl.ds(2 * m, 16, stride=8), :]
                b = turned[q, pl.ds(2 * m + 1, 16, stride=8), :]
                even = jnp.where(low, a, pltpu.roll(b, 64, 1))
                odd = jnp.where(low, pltpu.roll(a, 64, 1), b)
                primed[q * 32:q * 32 + 16, m * 128:m * 128 + 128] = even.astype(BF16)
                primed[q * 32 + 16:q * 32 + 32, m * 128:m * 128 + 128] = odd.astype(BF16)
        result[...] = rows_of(primed[...], order[0]).astype(BF16)

    def pair_copy(i):
        if i < 3:
            src = left_in.at[1 - core] if i == 0 else left.at[i - 1, 1 - core]
            dst = left_in.at[2] if i == 0 else left.at[i - 1, 2]
        else:
            cols = pl.ds(*((0, 1024), (1024, 1024), (2048, 512))[i - 3])
            src, dst = right.at[0, :, cols], right.at[1, :, cols]
        return pltpu.make_async_remote_copy(
            src_ref=src, dst_ref=dst, send_sem=pair_send.at[i], recv_sem=pair_recv.at[i],
            device_id=mate, device_id_type=MESH,
        )

    def layer(source, weights, slopes, which):
        def body(j, carry):
            cols = pl.ds(pl.multiple_of(j * 256, 256), 256)
            value, slope = gelu_pair(rows_of(source[...], weights[:, cols]))
            slopes[:, cols] = slope
            hidden[which, :, cols] = value.astype(BF16)
            flipped = value.T.astype(BF16)
            for x in range(4):
                for half in (0, 1):
                    left[which, half, pl.ds(pl.multiple_of((j * 4 + x) * 32, 32), 32), :] = flipped[
                        x * 64 + half * 32:x * 64 + half * 32 + 32, :
                    ]
            return carry

        lax.fori_loop(0, 4, body, 0)

    loads[2].wait()
    layer(inputs, wf, slope1, 0)
    pair_copy(1).start()
    for half in (0, 1):
        left_in[half] = rows_of_t(order[1 + half], inputs[...]).astype(BF16)
    pair_copy(0).start()
    loads[3].wait()
    layer(hidden.at[0], wm, slope2, 1)
    pair_copy(2).start()
    loads[4].wait()
    forcing = rows_of(hidden[1], wl[...])
    right[0, :, 2048:2560] = ((forcing - targets[...].astype(F32)) * (1.0 / 128)).astype(BF16)
    pair_copy(5).start()

    def backward(error_cols, weights, slopes, first_col):
        def body(j, carry):
            cols = pl.ds(pl.multiple_of(j * 256, 256), 256)
            carried = rows_of_t(right[0, :, error_cols], weights[cols, :])
            right[0, :, pl.ds(pl.multiple_of(first_col + j * 256, 256), 256)] = (
                carried * slopes[:, cols]
            ).astype(BF16)
            return carry

        lax.fori_loop(0, 4, body, 0)

    def stage(b, number, d):
        axis = "xy"[(b + number) % 2]
        if number == 0:
            src, dst, send, take = grad.at[b], recv1.at[b, d - 1], send1, take1
        else:
            src, dst, send, take = sum1.at[b], recv2.at[b, d - 1], send2, take2
        return pltpu.make_async_remote_copy(
            src_ref=src.at[(at[axis] + d) % 4], dst_ref=dst,
            send_sem=send.at[b, d - 1], recv_sem=take.at[b, d - 1],
            device_id=moved(at, axis, d), device_id_type=MESH,
        )

    def gradient(b, own, other, cols):
        both = jnp.concatenate([own, other], axis=1)
        columns = jnp.concatenate([right[0, :, cols], right[1, :, cols]], axis=0)
        return rows_of(both, columns)

    def keep(b, value):
        cut = value.reshape(4, 4, 4, 8, 256)
        for i in range(4):
            grad[b, i] = cut[:, i] if b % 2 == 0 else cut[:, :, i]
        for d in (1, 2, 3):
            stage(b, 0, d).start()

    backward(pl.ds(2048, 512), wl, slope2, 1024)
    pair_copy(4).start()
    pair_copy(2).wait_recv()
    pair_copy(5).wait_recv()
    for b in (0, 1):
        keep(b, gradient(b, left[1, core], left[1, 2], slice(2048 + b * 256, 2304 + b * 256)))

    top = forcing.astype(BF16)
    rest = forcing - top.astype(F32)
    middle = rest.astype(BF16)
    rest = (rest - middle.astype(F32)).astype(BF16)
    back = rows_of_t(top, order[0]) + rows_of_t(middle, order[0]) + rows_of_t(rest, order[0])
    for m in range(4):
        for q in range(4):
            even = back[q * 32:q * 32 + 16, m * 128:m * 128 + 128]
            odd = back[q * 32 + 16:q * 32 + 32, m * 128:m * 128 + 128]
            turned[q, pl.ds(2 * m, 16, stride=8), :] = jnp.where(low, even, pltpu.roll(odd, 64, 1))
            turned[q, pl.ds(2 * m + 1, 16, stride=8), :] = jnp.where(low, pltpu.roll(even, 64, 1), odd)
    for q in range(4):
        forced[q * 128:q * 128 + 128, :] = turned[q].T
    step(3, True)

    backward(pl.ds(1024, 1024), wm, slope1, 0)
    pair_copy(3).start()
    pair_copy(1).wait_recv()
    pair_copy(4).wait_recv()
    for b in (2, 3, 4, 5):
        col = 1024 + (b - 2) * 256
        keep(b, gradient(b, left[0, core], left[0, 2], slice(col, col + 256)))
    pair_copy(0).wait_recv()
    pair_copy(3).wait_recv()
    upper = (lax.broadcasted_iota(jnp.int32, (512, 256), 0) // 2) % 2 == 0
    for b in (6, 7):
        col = (b - 6) * 256
        keep(
            b,
            jnp.where(
                upper,
                gradient(b, left_in[core], left_in[2], slice(col, col + 256)),
                gradient(b, left_in[core], left_in[2], slice(col + 512, col + 768)),
            ),
        )

    step(4, True)

    sub = lax.broadcasted_iota(jnp.int32, (8, 128), 0) < 4

    def after_first(b):
        axis = "xy"[b % 2]
        for d in (1, 2, 3):
            stage(b, 0, d).wait_recv()
        total = grad[b, at[axis]] + recv1[b, 0] + recv1[b, 1] + recv1[b, 2]
        for i in range(4):
            sum1[b, i] = total[:, i]
        for d in (1, 2, 3):
            stage(b, 1, d).start()

    def after_second(b):
        axis = "xy"[(b + 1) % 2]
        for d in (1, 2, 3):
            stage(b, 1, d).wait_recv()
        total = sum1[b, at[axis]] + recv2[b, 0] + recv2[b, 1] + recv2[b, 2]
        for zh in range(4):
            lo, hi = total[zh, :, :128], total[zh, :, 128:]
            here = slice(b % 2 * 128, b % 2 * 128 + 128)
            pack[b // 2, 2 * zh, :, here] = jnp.where(sub, lo, pltpu.roll(hi, 4, 0))
            pack[b // 2, 2 * zh + 1, :, here] = jnp.where(sub, pltpu.roll(lo, 4, 0), hi)

    def stage3(piece, d):
        return pltpu.make_async_remote_copy(
            src_ref=pack.at[piece, (at["z"] + d) % 8], dst_ref=recv3.at[piece, d - 1],
            send_sem=send3.at[piece, d - 1], recv_sem=take3.at[piece, d - 1],
            device_id=moved(at, "z", d), device_id_type=MESH,
        )

    for b in range(BLOCKS):
        after_first(b)
    step(5, True)
    out = pltpu.make_async_copy(st.at[0, :, pl.ds(1, 16)], conc_out, out_sem)
    out.start()
    for b in range(BLOCKS):
        after_second(b)
        if b % 2 == 1:
            for d in range(1, 8):
                stage3(b // 2, d).start()
    for piece in range(4):
        for d in range(1, 8):
            stage3(piece, d).wait_recv()
        total = pack[piece, at["z"]]
        for d in range(7):
            total = total + recv3[piece, d]
        sums_out[:, piece * 256:piece * 256 + 256] = total

    out.wait()
    for i in range(6):
        pair_copy(i).wait_send()
    for b in range(BLOCKS):
        for d in (1, 2, 3):
            stage(b, 0, d).wait_send()
            stage(b, 1, d).wait_send()
    for piece in range(4):
        for d in range(1, 8):
            stage3(piece, d).wait_send()
    for copy in halo_copies((STEPS - 1) % 2):
        copy.wait_send()


def unpack(conc, sums, conc_out, gf_out, gm_out, gl_out, buffer, sem):
    into, onward = [], []
    for i in range(4):
        here = (i // 2, pl.ds(i % 2 * 8, 8))
        into.append(pltpu.make_async_copy(conc.at[here], buffer.at[here], sem.at[0, i]))
        onward.append(pltpu.make_async_copy(buffer.at[here], conc_out.at[here], sem.at[1, i]))
        into[-1].start()

    def wide(b):
        part = sums[:, b * 128:b * 128 + 128]
        return jnp.concatenate([part[0:4], part[4:8]], axis=1)

    gl_out[...] = jnp.concatenate([wide(0), wide(1)], axis=1)
    gm_out[...] = jnp.concatenate([wide(b) for b in (2, 3, 4, 5)], axis=1)
    whole = jnp.concatenate([wide(6), wide(7)], axis=1)
    gf_out[...] = jnp.concatenate([whole[0:2], whole[2:4]], axis=1)
    for i in range(4):
        into[i].wait()
        onward[i].start()
    for copy in onward:
        copy.wait()


def per_device(concentrations, diffusivity, weight_first, weight_middle, weight_last):
    any_space = pl.BlockSpec(memory_space=pl.ANY)
    vmem = pl.BlockSpec(memory_space=pltpu.VMEM)
    dma = pltpu.SemaphoreType.DMA
    state, sums = pl.pallas_call(
        kernel,
        out_shape=(
            jax.ShapeDtypeStruct((2, 16, 32, 128), F32),
            jax.ShapeDtypeStruct((8, BLOCKS * 128), F32),
        ),
        in_specs=[any_space] * 5,
        out_specs=(any_space, vmem),
        scratch_shapes=[
            pltpu.VMEM((2, 2, 18, 32, 128), F32),
            pltpu.VMEM((16, 32, 128), F32),
            pltpu.VMEM((2, 2, 2, 16, 128), F32),
            pltpu.VMEM((2, 32, 128), F32),
            pltpu.VMEM((2, 2, 2, 16, 128), F32),
            pltpu.VMEM((2, 32, 128), F32),
            pltpu.VMEM((512, 128), F32),
            pltpu.VMEM((512, 128), F32),
            pltpu.VMEM((4, 128, 128), F32),
            pltpu.VMEM((512, 128), F32),
            pltpu.VMEM((512, 1024), BF16),
            pltpu.VMEM((1024, 1024), BF16),
            pltpu.VMEM((1024, 512), BF16),
            pltpu.VMEM((3, 512, 512), BF16),
            pltpu.VMEM((128, 512), BF16),
            pltpu.VMEM((128, 512), BF16),
            pltpu.VMEM((128, 512), BF16),
            pltpu.VMEM((128, 1024), F32),
            pltpu.VMEM((128, 1024), F32),
            pltpu.VMEM((2, 128, 1024), BF16),
            pltpu.VMEM((2, 3, 512, 128), BF16),
            pltpu.VMEM((3, 512, 128), BF16),
            pltpu.VMEM((2, 128, 2560), BF16),
            pltpu.VMEM((BLOCKS, 4, 4, 4, 8, 256), F32),
            pltpu.VMEM((BLOCKS, 3, 4, 4, 8, 256), F32),
            pltpu.VMEM((BLOCKS, 4, 4, 8, 256), F32),
            pltpu.VMEM((BLOCKS, 3, 4, 8, 256), F32),
            pltpu.VMEM((4, 8, 8, 256), F32),
            pltpu.VMEM((4, 7, 8, 256), F32),
            dma((5,)), dma, dma((2, 5)), dma((2, 5)), dma((6,)), dma((6,)),
            dma((BLOCKS, 3)), dma((BLOCKS, 3)), dma((BLOCKS, 3)), dma((BLOCKS, 3)),
            dma((4, 7)), dma((4, 7)),
        ],
        compiler_params=pltpu.CompilerParams(
            collective_id=0, has_side_effects=True, vmem_limit_bytes=56 << 20
        ),
        name="whole_step",
    )(concentrations, diffusivity, weight_first, weight_middle, weight_last)
    return pl.pallas_call(
        unpack,
        out_shape=(
            jax.ShapeDtypeStruct((2, 16, 32, 128), F32),
            jax.ShapeDtypeStruct((2, 1024), F32),
            jax.ShapeDtypeStruct((4, 1024), F32),
            jax.ShapeDtypeStruct((4, 512), F32),
        ),
        in_specs=[any_space, vmem],
        out_specs=(any_space, vmem, vmem, vmem),
        scratch_shapes=[pltpu.VMEM((2, 16, 32, 128), F32), dma((2, 4))],
        name="outputs",
    )(state, sums)


def solution(mesh):
    in_specs = (P(None, "gx", "gy", "row"), P("gx", "gy", "row"), P(), P(), P())
    out_specs = (
        P(None, "gx", "gy", "row"),
        P(("gx", "gy", "row"), None),
        P(("gx", "gy", "row"), None),
        P(("gx", "gy", "row"), None),
    )
    return jax.shard_map(
        per_device, mesh=mesh, in_specs=in_specs, out_specs=out_specs, check_vma=False
    )
```

```python
import jax
import jax.numpy as jnp
from jax import lax
from jax.experimental import pallas as pl
from jax.experimental.pallas import tpu as pltpu
from jax.sharding import PartitionSpec as P

STEPS = 6
F32 = jnp.float32
BF16 = jnp.bfloat16
MESH = pl.DeviceIdType.MESH
BLOCKS = 8
HALVED = (1, 2)
SLOT = {0: 0, 1: 1, 6: 2, 7: 3, 2: 0, 3: 1, 4: 2, 5: 3}
GELU_A = 0.7978845608028654
GELU_B = 0.044715


def place():
    gx, gy, row = lax.axis_index("gx"), lax.axis_index("gy"), lax.axis_index("row")
    return {"core": gx % 2, "x": (gx // 2) % 4, "y": gy, "z": (gx // 8) * 2 + row}


def device(at):
    return {
        "gx": (at["z"] // 2) * 8 + at["x"] * 2 + at["core"],
        "gy": at["y"],
        "row": at["z"] % 2,
    }


def moved(at, axis, distance):
    size = {"core": 2, "x": 4, "y": 4, "z": 8}[axis]
    return device({**at, axis: (at[axis] + distance) % size})


def gelu_pair(values):
    squared = values * values
    bent = jnp.tanh(GELU_A * (values + GELU_B * (values * squared)))
    half = 0.5 * (1.0 + bent)
    slope = half + (0.5 * values) * (1.0 - bent * bent) * (
        GELU_A + (3.0 * GELU_A * GELU_B) * squared
    )
    return values * half, slope


def rows_of(left, right):
    return lax.dot_general(left, right, (((1,), (0,)), ((), ())), preferred_element_type=F32)


def rows_of_t(left, right):
    return lax.dot_general(left, right, (((1,), (1,)), ((), ())), preferred_element_type=F32)


def kernel(
    conc, diff_in, wf_in, wm_in, wl_in,
    conc_out, sums_out,
    st, diff, ysend, zsend, hy, hz, tiles_u, tiles_v, turned, forced,
    wf, wm, wl, order, primed, inputs, targets, slope1, slope2, hidden,
    left, left_in, right,
    grad, recv1, sum1, recv2, pack, recv3, hgrad, hrecv, hrecv1, hsum1, hrecv2, hpack, hrecv3,
    load_sem, out_sem, halo_send, halo_recv, pair_send, pair_recv,
    half_send, half_take, send1, take1, send2, take2, send3, take3,
):
    at = place()
    gx, gy, row = lax.axis_index("gx"), lax.axis_index("gy"), lax.axis_index("row")
    mate = moved(at, "core", 1)
    core = at["core"]

    loads = [
        pltpu.make_async_copy(conc, st.at[0, :, pl.ds(1, 16)], load_sem.at[0]),
        pltpu.make_async_copy(diff_in, diff, load_sem.at[1]),
        pltpu.make_async_copy(wf_in, wf, load_sem.at[2]),
        pltpu.make_async_copy(wm_in, wm, load_sem.at[3]),
        pltpu.make_async_copy(wl_in, wl, load_sem.at[4]),
    ]
    for copy in loads:
        copy.start()

    barrier = pltpu.get_barrier_semaphore()
    peers = [{"gx": (gx + 1) % 32}, {"gx": (gx + 31) % 32}]
    peers += [moved(at, "x", d) for d in (1, 2, 3)]
    peers += [moved(at, "y", d) for d in (1, 2, 3)]
    peers += [moved(at, "z", d) for d in range(1, 8)]
    for peer in peers:
        pl.semaphore_signal(barrier, inc=1, device_id=peer, device_id_type=MESH)

    iota_y = lax.broadcasted_iota(jnp.int32, (32, 128), 0)
    iota_z = lax.broadcasted_iota(jnp.int32, (32, 128), 1)
    pair_z = iota_z // 2

    def face_rows(par, x, new, packed):
        for f in (0, 1):
            ysend[par, 0, f, pl.ds(x, 1), :] = new[f][0:1, :]
            ysend[par, 1, f, pl.ds(x, 1), :] = new[f][31:32, :]
            k = f * 16 + x
            packed = jnp.where(pair_z == k, pltpu.roll(new[f], 2 * k + 1, 1), packed)
        return packed

    def halo_copies(par):
        plan = [
            (st.at[par, :, 1], st.at[par, :, 17], {"gx": (gx + 31) % 32}),
            (st.at[par, :, 16], st.at[par, :, 0], {"gx": (gx + 1) % 32}),
            (ysend.at[par, 0], hy.at[par, 1], {"gy": (gy + 3) % 4}),
            (ysend.at[par, 1], hy.at[par, 0], {"gy": (gy + 1) % 4}),
            (zsend.at[par], hz.at[par], {"row": 1 - row}),
        ]
        return [
            pltpu.make_async_remote_copy(
                src_ref=src, dst_ref=dst,
                send_sem=halo_send.at[par, i], recv_sem=halo_recv.at[par, i],
                device_id=who, device_id_type=MESH,
            )
            for i, (src, dst, who) in enumerate(plan)
        ]

    def step(number, force):
        par, nxt = number % 2, (number + 1) % 2
        for copy in halo_copies(par)[2:]:
            copy.wait_recv()
        if number >= 1:
            for copy in halo_copies(nxt):
                copy.wait_send()
        last = number == STEPS - 1

        def body(x, packed):
            hzv = hz[par]
            laps, centers = [], []
            for f in (0, 1):
                c = st[par, f, x + 1]
                y_next = hy[par, 1, f, pl.ds(x, 1), :]
                y_prev = hy[par, 0, f, pl.ds(x, 1), :]
                k = f * 16 + x
                yp = jnp.where(iota_y == 31, y_next, pltpu.roll(c, 31, 0))
                ym = jnp.where(iota_y == 0, y_prev, pltpu.roll(c, 1, 0))
                edges = pltpu.roll(hzv, 127 - 2 * k, 1)
                zp = pltpu.roll(jnp.where(iota_z == 0, edges, c), 127, 1)
                zm = pltpu.roll(jnp.where(iota_z == 127, edges, c), 1, 1)
                lap = -6.0 * c + st[par, f, x + 2] + st[par, f, x] + yp + ym + zp + zm
                laps.append(lap)
                centers.append(c)
            u, v = centers
            d = diff[x]
            product = u * v * v
            inner = d * laps[0] - product + 0.04 * (1.0 - u)
            if force:
                base = (x // 8) * 256 + (x % 8) * 8
                inner = inner + jnp.concatenate(
                    [forced[pl.ds(pl.multiple_of(base + py * 64, 8), 8), :] for py in range(4)], axis=0
                )
            new_u = u + 0.1 * inner
            new_v = v + 0.1 * (0.5 * d * laps[1] + product - 0.1 * v)
            st[nxt, 0, x + 1] = new_u
            st[nxt, 1, x + 1] = new_v
            if number == STEPS // 2 - 1:
                base = (x // 8) * 256 + (x % 8) * 8
                for py in range(4):
                    here = pl.ds(pl.multiple_of(base + py * 64, 8), 8)
                    tiles_u[here, :] = new_u[py * 8:py * 8 + 8, :]
                    tiles_v[here, :] = new_v[py * 8:py * 8 + 8, :]
            if last:
                return packed
            return face_rows(nxt, x, (new_u, new_v), packed)

        packed = lax.fori_loop(2, 14, body, jnp.zeros((32, 128), F32), unroll=4)
        for copy in halo_copies(par)[:2]:
            copy.wait_recv()
        for x in (0, 1, 14, 15):
            packed = body(x, packed)
        if not last:
            zsend[nxt] = packed
            for copy in halo_copies(nxt):
                copy.start()

    loads[0].wait()

    def first_faces(x, packed):
        return face_rows(0, x, (st[0, 0, x + 1], st[0, 1, x + 1]), packed)

    zsend[0] = lax.fori_loop(0, 16, first_faces, jnp.zeros((32, 128), F32), unroll=4)
    pl.semaphore_wait(barrier, len(peers))
    for copy in halo_copies(0):
        copy.start()

    r = lax.broadcasted_iota(jnp.int32, (512, 512), 0)
    c = lax.broadcasted_iota(jnp.int32, (512, 512), 1)
    order[0] = jnp.where(c == (r % 64) * 8 + r // 64, 1.0, 0.0).astype(BF16)
    for half in (0, 1):
        cell = (r // 128) * 128 + ((r // 32) % 4) * 32 + half * 16
        cell = cell + ((r // 8) % 4) * 4 + ((r // 4) % 2) * 2 + r % 2
        order[1 + half] = jnp.where(c == cell, 1.0, 0.0).astype(BF16)

    loads[1].wait()
    step(0, False)
    step(1, False)
    step(2, False)

    low = lax.broadcasted_iota(jnp.int32, (16, 128), 1) < 64
    for tiles, result in ((tiles_u, inputs), (tiles_v, targets)):
        for q in range(4):
            turned[q] = tiles[q * 128:q * 128 + 128, :].T
        for m in range(4):
            for q in range(4):
                a = turned[q, pl.ds(2 * m, 16, stride=8), :]
                b = turned[q, pl.ds(2 * m + 1, 16, stride=8), :]
                even = jnp.where(low, a, pltpu.roll(b, 64, 1))
                odd = jnp.where(low, pltpu.roll(a, 64, 1), b)
                primed[q * 32:q * 32 + 16, m * 128:m * 128 + 128] = even.astype(BF16)
                primed[q * 32 + 16:q * 32 + 32, m * 128:m * 128 + 128] = odd.astype(BF16)
        result[...] = rows_of(primed[...], order[0]).astype(BF16)

    def pair_copy(i):
        if i < 3:
            src = left_in.at[1 - core] if i == 0 else left.at[i - 1, 1 - core]
            dst = left_in.at[2] if i == 0 else left.at[i - 1, 2]
        else:
            cols = pl.ds(*((0, 1024), (1024, 1024), (2048, 512))[i - 3])
            src, dst = right.at[0, :, cols], right.at[1, :, cols]
        return pltpu.make_async_remote_copy(
            src_ref=src, dst_ref=dst, send_sem=pair_send.at[i], recv_sem=pair_recv.at[i],
            device_id=mate, device_id_type=MESH,
        )

    def layer(source, weights, slopes, which):
        def body(j, carry):
            cols = pl.ds(pl.multiple_of(j * 256, 256), 256)
            value, slope = gelu_pair(rows_of(source[...], weights[:, cols]))
            slopes[:, cols] = slope
            hidden[which, :, cols] = value.astype(BF16)
            flipped = value.T.astype(BF16)
            for x in range(4):
                for half in (0, 1):
                    left[which, half, pl.ds(pl.multiple_of((j * 4 + x) * 32, 32), 32), :] = flipped[
                        x * 64 + half * 32:x * 64 + half * 32 + 32, :
                    ]
            return carry

        lax.fori_loop(0, 4, body, 0)

    loads[2].wait()
    layer(inputs, wf, slope1, 0)
    pair_copy(1).start()
    for half in (0, 1):
        left_in[half] = rows_of_t(order[1 + half], inputs[...]).astype(BF16)
    pair_copy(0).start()
    loads[3].wait()
    layer(hidden.at[0], wm, slope2, 1)
    pair_copy(2).start()
    loads[4].wait()
    forcing = rows_of(hidden[1], wl[...])
    right[0, :, 2048:2560] = ((forcing - targets[...].astype(F32)) * (1.0 / 128)).astype(BF16)
    pair_copy(5).start()

    def backward(error_cols, weights, slopes, first_col):
        def body(j, carry):
            cols = pl.ds(pl.multiple_of(j * 256, 256), 256)
            carried = rows_of_t(right[0, :, error_cols], weights[cols, :])
            right[0, :, pl.ds(pl.multiple_of(first_col + j * 256, 256), 256)] = (
                carried * slopes[:, cols]
            ).astype(BF16)
            return carry

        lax.fori_loop(0, 4, body, 0)

    def is_halved(b):
        return b // 2 in HALVED

    def halving(b):
        distance = 1 + row * 6 if b % 2 == 0 else 7 - row * 6
        return pltpu.make_async_remote_copy(
            src_ref=hgrad.at[SLOT[b], 1 - row], dst_ref=hrecv.at[SLOT[b]],
            send_sem=half_send.at[SLOT[b]], recv_sem=half_take.at[SLOT[b]],
            device_id=moved(at, "z", distance), device_id_type=MESH,
        )

    def stage(b, number, d):
        axis, k = "xy"[(b + number) % 2], SLOT[b]
        if is_halved(b):
            src, dst = (hgrad.at[k, row], hrecv1) if number == 0 else (hsum1.at[k], hrecv2)
        else:
            src, dst = (grad.at[k], recv1) if number == 0 else (sum1.at[k], recv2)
        send, take = (send1, take1) if number == 0 else (send2, take2)
        return pltpu.make_async_remote_copy(
            src_ref=src.at[(at[axis] + d) % 4], dst_ref=dst.at[k, d - 1],
            send_sem=send.at[b, d - 1], recv_sem=take.at[b, d - 1],
            device_id=moved(at, axis, d), device_id_type=MESH,
        )

    def gradient(b, own, other, cols):
        both = jnp.concatenate([own, other], axis=1)
        columns = jnp.concatenate([right[0, :, cols], right[1, :, cols]], axis=0)
        return rows_of(both, columns)

    upper_half = lax.broadcasted_iota(jnp.int32, (64, 8, 128), 1) < 4

    def keep(b, value):
        tiles = value.reshape(64, 8, 256)
        lo, hi = tiles[:, :, :128], tiles[:, :, 128:]
        even = jnp.where(upper_half, lo, pltpu.roll(hi, 4, 1))
        odd = jnp.where(upper_half, pltpu.roll(lo, 4, 1), hi)
        for zl, part in ((0, even), (1, odd)):
            part = part.reshape(4, 4, 4, 8, 128)
            for i in range(4):
                cut = part[:, i] if b % 2 == 0 else part[:, :, i]
                if is_halved(b):
                    hgrad[SLOT[b], zl, i] = cut
                else:
                    grad[SLOT[b], i, :, zl] = cut
        if is_halved(b):
            halving(b).start()
        else:
            for d in (1, 2, 3):
                stage(b, 0, d).start()

    backward(pl.ds(2048, 512), wl, slope2, 1024)
    pair_copy(4).start()
    pair_copy(2).wait_recv()
    pair_copy(5).wait_recv()
    for b in (0, 1):
        keep(b, gradient(b, left[1, core], left[1, 2], slice(2048 + b * 256, 2304 + b * 256)))
    pair_copy(1).wait_recv()
    pair_copy(4).wait_recv()
    for b in (2, 3, 4, 5):
        col = 1024 + (b - 2) * 256
        keep(b, gradient(b, left[0, core], left[0, 2], slice(col, col + 256)))
    backward(pl.ds(1024, 1024), wm, slope1, 0)
    pair_copy(3).start()
    pair_copy(0).wait_recv()
    pair_copy(3).wait_recv()
    upper = (lax.broadcasted_iota(jnp.int32, (512, 256), 0) // 2) % 2 == 0
    for b in (6, 7):
        col = (b - 6) * 256
        keep(
            b,
            jnp.where(
                upper,
                gradient(b, left_in[core], left_in[2], slice(col, col + 256)),
                gradient(b, left_in[core], left_in[2], slice(col + 512, col + 768)),
            ),
        )

    top = forcing.astype(BF16)
    rest = forcing - top.astype(F32)
    middle = rest.astype(BF16)
    rest = (rest - middle.astype(F32)).astype(BF16)
    back = rows_of_t(top, order[0]) + rows_of_t(middle, order[0]) + rows_of_t(rest, order[0])
    for m in range(4):
        for q in range(4):
            even = back[q * 32:q * 32 + 16, m * 128:m * 128 + 128]
            odd = back[q * 32 + 16:q * 32 + 32, m * 128:m * 128 + 128]
            turned[q, pl.ds(2 * m, 16, stride=8), :] = jnp.where(low, even, pltpu.roll(odd, 64, 1))
            turned[q, pl.ds(2 * m + 1, 16, stride=8), :] = jnp.where(low, pltpu.roll(even, 64, 1), odd)
    for q in range(4):
        forced[q * 128:q * 128 + 128, :] = turned[q].T
    step(3, True)

    def after_half(b):
        halving(b).wait_recv()
        hgrad[SLOT[b], row] = hgrad[SLOT[b], row] + hrecv[SLOT[b]]
        for d in (1, 2, 3):
            stage(b, 0, d).start()

    def after_first(b):
        k, me = SLOT[b], at["xy"[b % 2]]
        for d in (1, 2, 3):
            stage(b, 0, d).wait_recv()
        if is_halved(b):
            total = hgrad[k, row, me] + hrecv1[k, 0] + hrecv1[k, 1] + hrecv1[k, 2]
            for i in range(4):
                hsum1[k, i] = total[:, i]
        else:
            total = grad[k, me] + recv1[k, 0] + recv1[k, 1] + recv1[k, 2]
            for i in range(4):
                sum1[k, i] = total[:, :, i]
        for d in (1, 2, 3):
            stage(b, 1, d).start()

    def after_second(b):
        k, me = SLOT[b], at["xy"[(b + 1) % 2]]
        for d in (1, 2, 3):
            stage(b, 1, d).wait_recv()
        here = slice(b % 2 * 128, b % 2 * 128 + 128)
        if is_halved(b):
            total = hsum1[k, me] + hrecv2[k, 0] + hrecv2[k, 1] + hrecv2[k, 2]
            hpack[k // 2, :, :, here] = total
        else:
            total = sum1[k, me] + recv2[k, 0] + recv2[k, 1] + recv2[k, 2]
            pack[k // 2, :, :, here] = total.reshape(8, 8, 128)

    def stage3(piece, d):
        k = SLOT[2 * piece] // 2
        if piece in HALVED:
            src, dst = hpack.at[k, (at["z"] // 2 + d) % 4], hrecv3.at[k, d - 1]
            who = moved(at, "z", 2 * d)
        else:
            src, dst = pack.at[k, (at["z"] + d) % 8], recv3.at[k, d - 1]
            who = moved(at, "z", d)
        return pltpu.make_async_remote_copy(
            src_ref=src, dst_ref=dst,
            send_sem=send3.at[piece, d - 1], recv_sem=take3.at[piece, d - 1],
            device_id=who, device_id_type=MESH,
        )

    def hops(piece):
        return range(1, 4) if piece in HALVED else range(1, 8)

    def last_stage(piece):
        after_second(2 * piece)
        after_second(2 * piece + 1)
        for d in hops(piece):
            stage3(piece, d).start()

    def finish(piece):
        for d in hops(piece):
            stage3(piece, d).wait_recv()
        k = SLOT[2 * piece] // 2
        total = hpack[k, at["z"] // 2] if piece in HALVED else pack[k, at["z"]]
        for d in hops(piece):
            total = total + (hrecv3[k, d - 1] if piece in HALVED else recv3[k, d - 1])
        sums_out[:, piece * 256:piece * 256 + 256] = total

    after_half(2)
    after_half(3)
    after_first(0)
    after_first(1)
    after_half(4)
    after_half(5)
    after_first(6)
    after_first(7)
    step(4, True)
    after_first(2)
    after_first(3)
    last_stage(0)
    after_first(4)
    after_first(5)
    last_stage(3)
    last_stage(1)
    step(5, True)
    out = pltpu.make_async_copy(st.at[0, :, pl.ds(1, 16)], conc_out, out_sem)
    out.start()
    last_stage(2)
    for piece in (0, 3, 1, 2):
        finish(piece)

    out.wait()
    for i in range(6):
        pair_copy(i).wait_send()
    for b in range(BLOCKS):
        for d in (1, 2, 3):
            stage(b, 0, d).wait_send()
            stage(b, 1, d).wait_send()
    for piece in range(4):
        for d in hops(piece):
            stage3(piece, d).wait_send()
    for b in range(BLOCKS):
        if is_halved(b):
            halving(b).wait_send()
    for copy in halo_copies((STEPS - 1) % 2):
        copy.wait_send()


def unpack(conc, sums, conc_out, gf_out, gm_out, gl_out, buffer, sem):
    into, onward = [], []
    for i in range(4):
        here = (i // 2, pl.ds(i % 2 * 8, 8))
        into.append(pltpu.make_async_copy(conc.at[here], buffer.at[here], sem.at[0, i]))
        onward.append(pltpu.make_async_copy(buffer.at[here], conc_out.at[here], sem.at[1, i]))
        into[-1].start()

    def wide(b):
        part = sums[:, b * 128:b * 128 + 128]
        return jnp.concatenate([part[0:4], part[4:8]], axis=1)

    gl_out[...] = jnp.concatenate([wide(0), wide(1)], axis=1)
    gm_out[...] = jnp.concatenate([wide(b) for b in (2, 3, 4, 5)], axis=1)
    whole = jnp.concatenate([wide(6), wide(7)], axis=1)
    gf_out[...] = jnp.concatenate([whole[0:2], whole[2:4]], axis=1)
    for i in range(4):
        into[i].wait()
        onward[i].start()
    for copy in onward:
        copy.wait()


def per_device(concentrations, diffusivity, weight_first, weight_middle, weight_last):
    any_space = pl.BlockSpec(memory_space=pl.ANY)
    vmem = pl.BlockSpec(memory_space=pltpu.VMEM)
    dma = pltpu.SemaphoreType.DMA
    state, sums = pl.pallas_call(
        kernel,
        out_shape=(
            jax.ShapeDtypeStruct((2, 16, 32, 128), F32),
            jax.ShapeDtypeStruct((8, BLOCKS * 128), F32),
        ),
        in_specs=[any_space] * 5,
        out_specs=(any_space, vmem),
        scratch_shapes=[
            pltpu.VMEM((2, 2, 18, 32, 128), F32),
            pltpu.VMEM((16, 32, 128), F32),
            pltpu.VMEM((2, 2, 2, 16, 128), F32),
            pltpu.VMEM((2, 32, 128), F32),
            pltpu.VMEM((2, 2, 2, 16, 128), F32),
            pltpu.VMEM((2, 32, 128), F32),
            pltpu.VMEM((512, 128), F32),
            pltpu.VMEM((512, 128), F32),
            pltpu.VMEM((4, 128, 128), F32),
            pltpu.VMEM((512, 128), F32),
            pltpu.VMEM((512, 1024), BF16),
            pltpu.VMEM((1024, 1024), BF16),
            pltpu.VMEM((1024, 512), BF16),
            pltpu.VMEM((3, 512, 512), BF16),
            pltpu.VMEM((128, 512), BF16),
            pltpu.VMEM((128, 512), BF16),
            pltpu.VMEM((128, 512), BF16),
            pltpu.VMEM((128, 1024), F32),
            pltpu.VMEM((128, 1024), F32),
            pltpu.VMEM((2, 128, 1024), BF16),
            pltpu.VMEM((2, 3, 512, 128), BF16),
            pltpu.VMEM((3, 512, 128), BF16),
            pltpu.VMEM((2, 128, 2560), BF16),
            pltpu.VMEM((4, 4, 4, 2, 4, 8, 128), F32),
            pltpu.VMEM((4, 3, 4, 2, 4, 8, 128), F32),
            pltpu.VMEM((4, 4, 4, 2, 8, 128), F32),
            pltpu.VMEM((4, 3, 4, 2, 8, 128), F32),
            pltpu.VMEM((2, 8, 8, 256), F32),
            pltpu.VMEM((2, 7, 8, 256), F32),
            pltpu.VMEM((4, 2, 4, 4, 4, 8, 128), F32),
            pltpu.VMEM((4, 4, 4, 4, 8, 128), F32),
            pltpu.VMEM((4, 3, 4, 4, 8, 128), F32),
            pltpu.VMEM((4, 4, 4, 8, 128), F32),
            pltpu.VMEM((4, 3, 4, 8, 128), F32),
            pltpu.VMEM((2, 4, 8, 256), F32),
            pltpu.VMEM((2, 3, 8, 256), F32),
            dma((5,)), dma, dma((2, 5)), dma((2, 5)), dma((6,)), dma((6,)),
            dma((4,)), dma((4,)),
            dma((BLOCKS, 3)), dma((BLOCKS, 3)), dma((BLOCKS, 3)), dma((BLOCKS, 3)),
            dma((4, 7)), dma((4, 7)),
        ],
        compiler_params=pltpu.CompilerParams(
            collective_id=0, has_side_effects=True, vmem_limit_bytes=56 << 20
        ),
        name="whole_step",
    )(concentrations, diffusivity, weight_first, weight_middle, weight_last)
    return pl.pallas_call(
        unpack,
        out_shape=(
            jax.ShapeDtypeStruct((2, 16, 32, 128), F32),
            jax.ShapeDtypeStruct((2, 1024), F32),
            jax.ShapeDtypeStruct((4, 1024), F32),
            jax.ShapeDtypeStruct((4, 512), F32),
        ),
        in_specs=[any_space, vmem],
        out_specs=(any_space, vmem, vmem, vmem),
        scratch_shapes=[pltpu.VMEM((2, 16, 32, 128), F32), dma((2, 4))],
        name="outputs",
    )(state, sums)


def solution(mesh):
    in_specs = (P(None, "gx", "gy", "row"), P("gx", "gy", "row"), P(), P(), P())
    out_specs = (
        P(None, "gx", "gy", "row"),
        P(("gx", "gy", "row"), None),
        P(("gx", "gy", "row"), None),
        P(("gx", "gy", "row"), None),
    )
    return jax.shard_map(
        per_device, mesh=mesh, in_specs=in_specs, out_specs=out_specs, check_vma=False
    )
```

```python
import jax
import jax.numpy as jnp
from jax import lax
from jax.experimental import pallas as pl
from jax.experimental.pallas import tpu as pltpu
from jax.sharding import PartitionSpec as P

STEPS = 6
F32 = jnp.float32
BF16 = jnp.bfloat16
MESH = pl.DeviceIdType.MESH
BLOCKS = 8
HALVED = (1, 2)
SLOT = {0: 0, 1: 1, 6: 2, 7: 3, 2: 0, 3: 1, 4: 2, 5: 3}
GELU_A = 0.7978845608028654
GELU_B = 0.044715


def place():
    gx, gy, row = lax.axis_index("gx"), lax.axis_index("gy"), lax.axis_index("row")
    return {"core": gx % 2, "x": (gx // 2) % 4, "y": gy, "z": (gx // 8) * 2 + row}


def device(at):
    return {
        "gx": (at["z"] // 2) * 8 + at["x"] * 2 + at["core"],
        "gy": at["y"],
        "row": at["z"] % 2,
    }


def moved(at, axis, distance):
    size = {"core": 2, "x": 4, "y": 4, "z": 8}[axis]
    return device({**at, axis: (at[axis] + distance) % size})


def gelu_pair(values):
    squared = values * values
    bent = jnp.tanh(GELU_A * (values + GELU_B * (values * squared)))
    half = 0.5 * (1.0 + bent)
    slope = half + (0.5 * values) * (1.0 - bent * bent) * (
        GELU_A + (3.0 * GELU_A * GELU_B) * squared
    )
    return values * half, slope


def rows_of(left, right):
    return lax.dot_general(left, right, (((1,), (0,)), ((), ())), preferred_element_type=F32)


def rows_of_t(left, right):
    return lax.dot_general(left, right, (((1,), (1,)), ((), ())), preferred_element_type=F32)


def kernel(
    conc, diff_in, wf_in, wm_in, wl_in,
    conc_out, sums_out,
    st, diff, ysend, zsend, hy, hz, tiles_u, tiles_v, turned, forced,
    wf, wm, wl, order, primed, inputs, targets, slope1, slope2, hidden,
    left, left_in, right,
    grad, recv1, sum1, recv2, pack, recv3, hgrad, hrecv, hrecv1, hsum1, hrecv2, hpack, hrecv3,
    load_sem, out_sem, halo_send, halo_recv, pair_send, pair_recv,
    half_send, half_take, send1, take1, send2, take2, send3, take3,
):
    at = place()
    gx, gy, row = lax.axis_index("gx"), lax.axis_index("gy"), lax.axis_index("row")
    mate = moved(at, "core", 1)
    core = at["core"]

    loads = [
        pltpu.make_async_copy(conc, st.at[0, :, pl.ds(1, 16)], load_sem.at[0]),
        pltpu.make_async_copy(diff_in, diff, load_sem.at[1]),
        pltpu.make_async_copy(wf_in, wf, load_sem.at[2]),
        pltpu.make_async_copy(wm_in, wm, load_sem.at[3]),
        pltpu.make_async_copy(wl_in, wl, load_sem.at[4]),
    ]
    for copy in loads:
        copy.start()

    barrier = pltpu.get_barrier_semaphore()
    peers = [{"gx": (gx + 1) % 32}, {"gx": (gx + 31) % 32}]
    peers += [moved(at, "x", d) for d in (1, 2, 3)]
    peers += [moved(at, "y", d) for d in (1, 2, 3)]
    peers += [moved(at, "z", d) for d in range(1, 8)]
    for peer in peers:
        pl.semaphore_signal(barrier, inc=1, device_id=peer, device_id_type=MESH)

    iota_y = lax.broadcasted_iota(jnp.int32, (32, 128), 0)
    iota_z = lax.broadcasted_iota(jnp.int32, (32, 128), 1)
    pair_z = iota_z // 2

    def face_rows(par, x, new, packed):
        for f in (0, 1):
            ysend[par, 0, f, pl.ds(x, 1), :] = new[f][0:1, :]
            ysend[par, 1, f, pl.ds(x, 1), :] = new[f][31:32, :]
            k = f * 16 + x
            packed = jnp.where(pair_z == k, pltpu.roll(new[f], 2 * k + 1, 1), packed)
        return packed

    def halo_copies(par):
        plan = [
            (st.at[par, :, 1], st.at[par, :, 17], {"gx": (gx + 31) % 32}),
            (st.at[par, :, 16], st.at[par, :, 0], {"gx": (gx + 1) % 32}),
            (ysend.at[par, 0], hy.at[par, 1], {"gy": (gy + 3) % 4}),
            (ysend.at[par, 1], hy.at[par, 0], {"gy": (gy + 1) % 4}),
            (zsend.at[par], hz.at[par], {"row": 1 - row}),
        ]
        return [
            pltpu.make_async_remote_copy(
                src_ref=src, dst_ref=dst,
                send_sem=halo_send.at[par, i], recv_sem=halo_recv.at[par, i],
                device_id=who, device_id_type=MESH,
            )
            for i, (src, dst, who) in enumerate(plan)
        ]

    def step(number, force):
        par, nxt = number % 2, (number + 1) % 2
        for copy in halo_copies(par)[2:]:
            copy.wait_recv()
        if number >= 1:
            for copy in halo_copies(nxt):
                copy.wait_send()
        last = number == STEPS - 1

        def body(x, packed):
            hzv = hz[par]
            laps, centers = [], []
            for f in (0, 1):
                c = st[par, f, x + 1]
                y_next = hy[par, 1, f, pl.ds(x, 1), :]
                y_prev = hy[par, 0, f, pl.ds(x, 1), :]
                k = f * 16 + x
                yp = jnp.where(iota_y == 31, y_next, pltpu.roll(c, 31, 0))
                ym = jnp.where(iota_y == 0, y_prev, pltpu.roll(c, 1, 0))
                edges = pltpu.roll(hzv, 127 - 2 * k, 1)
                zp = pltpu.roll(jnp.where(iota_z == 0, edges, c), 127, 1)
                zm = pltpu.roll(jnp.where(iota_z == 127, edges, c), 1, 1)
                lap = -6.0 * c + st[par, f, x + 2] + st[par, f, x] + yp + ym + zp + zm
                laps.append(lap)
                centers.append(c)
            u, v = centers
            d = diff[x]
            product = u * v * v
            inner = d * laps[0] - product + 0.04 * (1.0 - u)
            if force:
                base = (x // 8) * 256 + (x % 8) * 8
                inner = inner + jnp.concatenate(
                    [forced[pl.ds(pl.multiple_of(base + py * 64, 8), 8), :] for py in range(4)], axis=0
                )
            new_u = u + 0.1 * inner
            new_v = v + 0.1 * (0.5 * d * laps[1] + product - 0.1 * v)
            st[nxt, 0, x + 1] = new_u
            st[nxt, 1, x + 1] = new_v
            if number == STEPS // 2 - 1:
                base = (x // 8) * 256 + (x % 8) * 8
                for py in range(4):
                    here = pl.ds(pl.multiple_of(base + py * 64, 8), 8)
                    tiles_u[here, :] = new_u[py * 8:py * 8 + 8, :]
                    tiles_v[here, :] = new_v[py * 8:py * 8 + 8, :]
            if last:
                return packed
            return face_rows(nxt, x, (new_u, new_v), packed)

        packed = lax.fori_loop(2, 14, body, jnp.zeros((32, 128), F32), unroll=4)
        for copy in halo_copies(par)[:2]:
            copy.wait_recv()
        for x in (0, 1, 14, 15):
            packed = body(x, packed)
        if not last:
            zsend[nxt] = packed
            for copy in halo_copies(nxt):
                copy.start()

    loads[0].wait()

    def first_faces(x, packed):
        return face_rows(0, x, (st[0, 0, x + 1], st[0, 1, x + 1]), packed)

    zsend[0] = lax.fori_loop(0, 16, first_faces, jnp.zeros((32, 128), F32), unroll=4)
    pl.semaphore_wait(barrier, len(peers))
    for copy in halo_copies(0):
        copy.start()

    r = lax.broadcasted_iota(jnp.int32, (512, 512), 0)
    c = lax.broadcasted_iota(jnp.int32, (512, 512), 1)
    order[0] = jnp.where(c == (r % 64) * 8 + r // 64, 1.0, 0.0).astype(BF16)
    for half in (0, 1):
        cell = (r // 128) * 128 + ((r // 32) % 4) * 32 + half * 16
        cell = cell + ((r // 8) % 4) * 4 + ((r // 4) % 2) * 2 + r % 2
        order[1 + half] = jnp.where(c == cell, 1.0, 0.0).astype(BF16)

    loads[1].wait()
    step(0, False)
    step(1, False)
    step(2, False)

    low = lax.broadcasted_iota(jnp.int32, (16, 128), 1) < 64
    for tiles, result in ((tiles_u, inputs), (tiles_v, targets)):
        for q in range(4):
            turned[q] = tiles[q * 128:q * 128 + 128, :].T
        for m in range(4):
            for q in range(4):
                a = turned[q, pl.ds(2 * m, 16, stride=8), :]
                b = turned[q, pl.ds(2 * m + 1, 16, stride=8), :]
                even = jnp.where(low, a, pltpu.roll(b, 64, 1))
                odd = jnp.where(low, pltpu.roll(a, 64, 1), b)
                primed[q * 32:q * 32 + 16, m * 128:m * 128 + 128] = even.astype(BF16)
                primed[q * 32 + 16:q * 32 + 32, m * 128:m * 128 + 128] = odd.astype(BF16)
        result[...] = rows_of(primed[...], order[0]).astype(BF16)

    def pair_copy(i):
        if i < 3:
            src = left_in.at[1 - core] if i == 0 else left.at[i - 1, 1 - core]
            dst = left_in.at[2] if i == 0 else left.at[i - 1, 2]
        else:
            cols = pl.ds(*((0, 1024), (1024, 1024), (2048, 512))[i - 3])
            src, dst = right.at[0, :, cols], right.at[1, :, cols]
        return pltpu.make_async_remote_copy(
            src_ref=src, dst_ref=dst, send_sem=pair_send.at[i], recv_sem=pair_recv.at[i],
            device_id=mate, device_id_type=MESH,
        )

    def layer(source, weights, slopes, which):
        def body(j, carry):
            cols = pl.ds(pl.multiple_of(j * 256, 256), 256)
            value, slope = gelu_pair(rows_of(source[...], weights[:, cols]))
            slopes[:, cols] = slope
            hidden[which, :, cols] = value.astype(BF16)
            flipped = value.T.astype(BF16)
            for x in range(4):
                for half in (0, 1):
                    left[which, half, pl.ds(pl.multiple_of((j * 4 + x) * 32, 32), 32), :] = flipped[
                        x * 64 + half * 32:x * 64 + half * 32 + 32, :
                    ]
            return carry

        lax.fori_loop(0, 4, body, 0, unroll=4)

    loads[2].wait()
    layer(inputs, wf, slope1, 0)
    pair_copy(1).start()
    for half in (0, 1):
        left_in[half] = rows_of_t(order[1 + half], inputs[...]).astype(BF16)
    pair_copy(0).start()
    loads[3].wait()
    layer(hidden.at[0], wm, slope2, 1)
    pair_copy(2).start()
    loads[4].wait()
    forcing = rows_of(hidden[1], wl[...])
    right[0, :, 2048:2560] = ((forcing - targets[...].astype(F32)) * (1.0 / 128)).astype(BF16)
    pair_copy(5).start()

    def backward(error_cols, weights, slopes, first_col):
        def body(j, carry):
            cols = pl.ds(pl.multiple_of(j * 256, 256), 256)
            carried = rows_of_t(right[0, :, error_cols], weights[cols, :])
            right[0, :, pl.ds(pl.multiple_of(first_col + j * 256, 256), 256)] = (
                carried * slopes[:, cols]
            ).astype(BF16)
            return carry

        lax.fori_loop(0, 4, body, 0, unroll=4)

    def is_halved(b):
        return b // 2 in HALVED

    def halving(b):
        distance = 1 + row * 6 if b % 2 == 0 else 7 - row * 6
        return pltpu.make_async_remote_copy(
            src_ref=hgrad.at[SLOT[b], 1 - row], dst_ref=hrecv.at[SLOT[b]],
            send_sem=half_send.at[SLOT[b]], recv_sem=half_take.at[SLOT[b]],
            device_id=moved(at, "z", distance), device_id_type=MESH,
        )

    def stage(b, number, d):
        axis, k = "xy"[(b + number) % 2], SLOT[b]
        if is_halved(b):
            src, dst = (hgrad.at[k, row], hrecv1) if number == 0 else (hsum1.at[k], hrecv2)
        else:
            src, dst = (grad.at[k], recv1) if number == 0 else (sum1.at[k], recv2)
        send, take = (send1, take1) if number == 0 else (send2, take2)
        return pltpu.make_async_remote_copy(
            src_ref=src.at[(at[axis] + d) % 4], dst_ref=dst.at[k, d - 1],
            send_sem=send.at[b, d - 1], recv_sem=take.at[b, d - 1],
            device_id=moved(at, axis, d), device_id_type=MESH,
        )

    def gradient(b, own, other, cols):
        both = jnp.concatenate([own, other], axis=1)
        columns = jnp.concatenate([right[0, :, cols], right[1, :, cols]], axis=0)
        return rows_of(both, columns)

    upper_half = lax.broadcasted_iota(jnp.int32, (64, 8, 128), 1) < 4

    def keep(b, value):
        tiles = value.reshape(64, 8, 256)
        lo, hi = tiles[:, :, :128], tiles[:, :, 128:]
        even = jnp.where(upper_half, lo, pltpu.roll(hi, 4, 1))
        odd = jnp.where(upper_half, pltpu.roll(lo, 4, 1), hi)
        for zl, part in ((0, even), (1, odd)):
            part = part.reshape(4, 4, 4, 8, 128)
            for i in range(4):
                cut = part[:, i] if b % 2 == 0 else part[:, :, i]
                if is_halved(b):
                    hgrad[SLOT[b], zl, i] = cut
                else:
                    grad[SLOT[b], i, :, zl] = cut
        if is_halved(b):
            halving(b).start()
        else:
            for d in (1, 2, 3):
                stage(b, 0, d).start()

    backward(pl.ds(2048, 512), wl, slope2, 1024)
    pair_copy(4).start()
    pair_copy(2).wait_recv()
    pair_copy(5).wait_recv()
    for b in (0, 1):
        keep(b, gradient(b, left[1, core], left[1, 2], slice(2048 + b * 256, 2304 + b * 256)))
    pair_copy(1).wait_recv()
    pair_copy(4).wait_recv()
    for b in (2, 3, 4, 5):
        col = 1024 + (b - 2) * 256
        keep(b, gradient(b, left[0, core], left[0, 2], slice(col, col + 256)))
    backward(pl.ds(1024, 1024), wm, slope1, 0)
    pair_copy(3).start()
    pair_copy(0).wait_recv()
    pair_copy(3).wait_recv()
    upper = (lax.broadcasted_iota(jnp.int32, (512, 256), 0) // 2) % 2 == 0
    for b in (6, 7):
        col = (b - 6) * 256
        keep(
            b,
            jnp.where(
                upper,
                gradient(b, left_in[core], left_in[2], slice(col, col + 256)),
                gradient(b, left_in[core], left_in[2], slice(col + 512, col + 768)),
            ),
        )

    top = forcing.astype(BF16)
    rest = forcing - top.astype(F32)
    middle = rest.astype(BF16)
    rest = (rest - middle.astype(F32)).astype(BF16)
    back = rows_of_t(top, order[0]) + rows_of_t(middle, order[0]) + rows_of_t(rest, order[0])
    for m in range(4):
        for q in range(4):
            even = back[q * 32:q * 32 + 16, m * 128:m * 128 + 128]
            odd = back[q * 32 + 16:q * 32 + 32, m * 128:m * 128 + 128]
            turned[q, pl.ds(2 * m, 16, stride=8), :] = jnp.where(low, even, pltpu.roll(odd, 64, 1))
            turned[q, pl.ds(2 * m + 1, 16, stride=8), :] = jnp.where(low, pltpu.roll(even, 64, 1), odd)
    for q in range(4):
        forced[q * 128:q * 128 + 128, :] = turned[q].T
    step(3, True)

    def after_half(b):
        halving(b).wait_recv()
        hgrad[SLOT[b], row] = hgrad[SLOT[b], row] + hrecv[SLOT[b]]
        for d in (1, 2, 3):
            stage(b, 0, d).start()

    def after_first(b):
        k, me = SLOT[b], at["xy"[b % 2]]
        for d in (1, 2, 3):
            stage(b, 0, d).wait_recv()
        if is_halved(b):
            total = hgrad[k, row, me] + hrecv1[k, 0] + hrecv1[k, 1] + hrecv1[k, 2]
            for i in range(4):
                hsum1[k, i] = total[:, i]
        else:
            total = grad[k, me] + recv1[k, 0] + recv1[k, 1] + recv1[k, 2]
            for i in range(4):
                sum1[k, i] = total[:, :, i]
        for d in (1, 2, 3):
            stage(b, 1, d).start()

    def after_second(b):
        k, me = SLOT[b], at["xy"[(b + 1) % 2]]
        for d in (1, 2, 3):
            stage(b, 1, d).wait_recv()
        here = slice(b % 2 * 128, b % 2 * 128 + 128)
        if is_halved(b):
            total = hsum1[k, me] + hrecv2[k, 0] + hrecv2[k, 1] + hrecv2[k, 2]
            hpack[k // 2, :, :, here] = total
        else:
            total = sum1[k, me] + recv2[k, 0] + recv2[k, 1] + recv2[k, 2]
            pack[k // 2, :, :, here] = total.reshape(8, 8, 128)

    def stage3(piece, d):
        k = SLOT[2 * piece] // 2
        if piece in HALVED:
            src, dst = hpack.at[k, (at["z"] // 2 + d) % 4], hrecv3.at[k, d - 1]
            who = moved(at, "z", 2 * d)
        else:
            src, dst = pack.at[k, (at["z"] + d) % 8], recv3.at[k, d - 1]
            who = moved(at, "z", d)
        return pltpu.make_async_remote_copy(
            src_ref=src, dst_ref=dst,
            send_sem=send3.at[piece, d - 1], recv_sem=take3.at[piece, d - 1],
            device_id=who, device_id_type=MESH,
        )

    def hops(piece):
        return range(1, 4) if piece in HALVED else range(1, 8)

    def last_stage(piece):
        after_second(2 * piece)
        after_second(2 * piece + 1)
        for d in hops(piece):
            stage3(piece, d).start()

    def finish(piece):
        for d in hops(piece):
            stage3(piece, d).wait_recv()
        k = SLOT[2 * piece] // 2
        total = hpack[k, at["z"] // 2] if piece in HALVED else pack[k, at["z"]]
        for d in hops(piece):
            total = total + (hrecv3[k, d - 1] if piece in HALVED else recv3[k, d - 1])
        sums_out[:, piece * 256:piece * 256 + 256] = total

    after_half(2)
    after_half(3)
    after_first(0)
    after_first(1)
    after_half(4)
    after_half(5)
    after_first(6)
    after_first(7)
    step(4, True)
    after_first(2)
    after_first(3)
    last_stage(0)
    after_first(4)
    after_first(5)
    last_stage(3)
    last_stage(1)
    step(5, True)
    out = pltpu.make_async_copy(st.at[0, :, pl.ds(1, 16)], conc_out, out_sem)
    out.start()
    last_stage(2)
    for piece in (0, 3, 1, 2):
        finish(piece)

    out.wait()
    for i in range(6):
        pair_copy(i).wait_send()
    for b in range(BLOCKS):
        for d in (1, 2, 3):
            stage(b, 0, d).wait_send()
            stage(b, 1, d).wait_send()
    for piece in range(4):
        for d in hops(piece):
            stage3(piece, d).wait_send()
    for b in range(BLOCKS):
        if is_halved(b):
            halving(b).wait_send()
    for copy in halo_copies((STEPS - 1) % 2):
        copy.wait_send()


def unpack(sums, gf_out, gm_out, gl_out):
    def wide(b):
        part = sums[:, b * 128:b * 128 + 128]
        return jnp.concatenate([part[0:4], part[4:8]], axis=1)

    gl_out[...] = jnp.concatenate([wide(0), wide(1)], axis=1)
    gm_out[...] = jnp.concatenate([wide(b) for b in (2, 3, 4, 5)], axis=1)
    whole = jnp.concatenate([wide(6), wide(7)], axis=1)
    gf_out[...] = jnp.concatenate([whole[0:2], whole[2:4]], axis=1)


def per_device(concentrations, diffusivity, weight_first, weight_middle, weight_last):
    any_space = pl.BlockSpec(memory_space=pl.ANY)
    vmem = pl.BlockSpec(memory_space=pltpu.VMEM)
    dma = pltpu.SemaphoreType.DMA
    state, sums = pl.pallas_call(
        kernel,
        out_shape=(
            pltpu.VMEM((2, 16, 32, 128), F32),
            jax.ShapeDtypeStruct((8, BLOCKS * 128), F32),
        ),
        in_specs=[any_space] * 5,
        out_specs=(vmem, vmem),
        scratch_shapes=[
            pltpu.VMEM((2, 2, 18, 32, 128), F32),
            pltpu.VMEM((16, 32, 128), F32),
            pltpu.VMEM((2, 2, 2, 16, 128), F32),
            pltpu.VMEM((2, 32, 128), F32),
            pltpu.VMEM((2, 2, 2, 16, 128), F32),
            pltpu.VMEM((2, 32, 128), F32),
            pltpu.VMEM((512, 128), F32),
            pltpu.VMEM((512, 128), F32),
            pltpu.VMEM((4, 128, 128), F32),
            pltpu.VMEM((512, 128), F32),
            pltpu.VMEM((512, 1024), BF16),
            pltpu.VMEM((1024, 1024), BF16),
            pltpu.VMEM((1024, 512), BF16),
            pltpu.VMEM((3, 512, 512), BF16),
            pltpu.VMEM((128, 512), BF16),
            pltpu.VMEM((128, 512), BF16),
            pltpu.VMEM((128, 512), BF16),
            pltpu.VMEM((128, 1024), F32),
            pltpu.VMEM((128, 1024), F32),
            pltpu.VMEM((2, 128, 1024), BF16),
            pltpu.VMEM((2, 3, 512, 128), BF16),
            pltpu.VMEM((3, 512, 128), BF16),
            pltpu.VMEM((2, 128, 2560), BF16),
            pltpu.VMEM((4, 4, 4, 2, 4, 8, 128), F32),
            pltpu.VMEM((4, 3, 4, 2, 4, 8, 128), F32),
            pltpu.VMEM((4, 4, 4, 2, 8, 128), F32),
            pltpu.VMEM((4, 3, 4, 2, 8, 128), F32),
            pltpu.VMEM((2, 8, 8, 256), F32),
            pltpu.VMEM((2, 7, 8, 256), F32),
            pltpu.VMEM((4, 2, 4, 4, 4, 8, 128), F32),
            pltpu.VMEM((4, 4, 4, 4, 8, 128), F32),
            pltpu.VMEM((4, 3, 4, 4, 8, 128), F32),
            pltpu.VMEM((4, 4, 4, 8, 128), F32),
            pltpu.VMEM((4, 3, 4, 8, 128), F32),
            pltpu.VMEM((2, 4, 8, 256), F32),
            pltpu.VMEM((2, 3, 8, 256), F32),
            dma((5,)), dma, dma((2, 5)), dma((2, 5)), dma((6,)), dma((6,)),
            dma((4,)), dma((4,)),
            dma((BLOCKS, 3)), dma((BLOCKS, 3)), dma((BLOCKS, 3)), dma((BLOCKS, 3)),
            dma((4, 7)), dma((4, 7)),
        ],
        compiler_params=pltpu.CompilerParams(
            collective_id=0, has_side_effects=True, vmem_limit_bytes=56 << 20
        ),
        name="whole_step",
    )(concentrations, diffusivity, weight_first, weight_middle, weight_last)
    grads = pl.pallas_call(
        unpack,
        out_shape=(
            jax.ShapeDtypeStruct((2, 1024), F32),
            jax.ShapeDtypeStruct((4, 1024), F32),
            jax.ShapeDtypeStruct((4, 512), F32),
        ),
        in_specs=[vmem],
        out_specs=(vmem, vmem, vmem),
        name="outputs",
    )(sums)
    return (state, *grads)


def solution(mesh):
    in_specs = (P(None, "gx", "gy", "row"), P("gx", "gy", "row"), P(), P(), P())
    out_specs = (
        P(None, "gx", "gy", "row"),
        P(("gx", "gy", "row"), None),
        P(("gx", "gy", "row"), None),
        P(("gx", "gy", "row"), None),
    )
    return jax.shard_map(
        per_device, mesh=mesh, in_specs=in_specs, out_specs=out_specs, check_vma=False
    )
```

```python
import jax
import jax.numpy as jnp
from jax import lax
from jax.experimental import pallas as pl
from jax.experimental.pallas import tpu as pltpu
from jax.sharding import PartitionSpec as P

STEPS = 6
F32 = jnp.float32
BF16 = jnp.bfloat16
MESH = pl.DeviceIdType.MESH
BLOCKS = 8
HALVED = (1, 2)
SLOT = {0: 0, 1: 1, 6: 2, 7: 3, 2: 0, 3: 1, 4: 2, 5: 3}
GELU_A = 0.7978845608028654
GELU_B = 0.044715


def place():
    gx, gy, row = lax.axis_index("gx"), lax.axis_index("gy"), lax.axis_index("row")
    return {"core": gx % 2, "x": (gx // 2) % 4, "y": gy, "z": (gx // 8) * 2 + row}


def device(at):
    return {
        "gx": (at["z"] // 2) * 8 + at["x"] * 2 + at["core"],
        "gy": at["y"],
        "row": at["z"] % 2,
    }


def moved(at, axis, distance):
    size = {"core": 2, "x": 4, "y": 4, "z": 8}[axis]
    return device({**at, axis: (at[axis] + distance) % size})


def gelu_pair(values):
    squared = values * values
    bent = jnp.tanh(GELU_A * (values + GELU_B * (values * squared)))
    half = 0.5 * (1.0 + bent)
    slope = half + (0.5 * values) * (1.0 - bent * bent) * (
        GELU_A + (3.0 * GELU_A * GELU_B) * squared
    )
    return values * half, slope


def rows_of(left, right):
    return lax.dot_general(left, right, (((1,), (0,)), ((), ())), preferred_element_type=F32)


def rows_of_t(left, right):
    return lax.dot_general(left, right, (((1,), (1,)), ((), ())), preferred_element_type=F32)


def kernel(
    conc, diff_in, wf_in, wm_in, wl_in,
    conc_out, sums_out,
    st, diff, ysend, zsend, hy, hz, tiles_u, tiles_v, turned, forced,
    wf, wm, wl, order, primed, inputs, targets, slope1, slope2, hidden,
    left, left_in, right,
    grad, recv1, sum1, recv2, pack, recv3, hgrad, hrecv, hrecv1, hsum1, hrecv2, hpack, hrecv3,
    load_sem, out_sem, halo_send, halo_recv, pair_send, pair_recv,
    near, far, half_send, half_take, send1, take1, send2, take2, send3, take3,
):
    at = place()
    gx, gy, row = lax.axis_index("gx"), lax.axis_index("gy"), lax.axis_index("row")
    mate = moved(at, "core", 1)
    core = at["core"]

    loads = [
        pltpu.make_async_copy(conc, st.at[0, :, pl.ds(1, 16)], load_sem.at[0]),
        pltpu.make_async_copy(diff_in, diff, load_sem.at[1]),
        pltpu.make_async_copy(wf_in, wf, load_sem.at[2]),
        pltpu.make_async_copy(wm_in, wm, load_sem.at[3]),
        pltpu.make_async_copy(wl_in, wl, load_sem.at[4]),
    ]
    for copy in loads:
        copy.start()

    barrier = pltpu.get_barrier_semaphore()
    peers = [{"gx": (gx + 1) % 32}, {"gx": (gx + 31) % 32}]
    peers += [moved(at, "x", d) for d in (1, 2, 3)]
    peers += [moved(at, "y", d) for d in (1, 2, 3)]
    peers += [moved(at, "z", d) for d in (1, 7)]
    for peer in peers:
        pl.semaphore_signal(barrier, inc=1, device_id=peer, device_id_type=MESH)

    iota_y = lax.broadcasted_iota(jnp.int32, (32, 128), 0)
    iota_z = lax.broadcasted_iota(jnp.int32, (32, 128), 1)
    pair_z = iota_z // 2

    def face_rows(par, x, new, packed):
        for f in (0, 1):
            ysend[par, 0, f, pl.ds(x, 1), :] = new[f][0:1, :]
            ysend[par, 1, f, pl.ds(x, 1), :] = new[f][31:32, :]
            k = f * 16 + x
            packed = jnp.where(pair_z == k, pltpu.roll(new[f], 2 * k + 1, 1), packed)
        return packed

    def halo_copies(par):
        plan = [
            (st.at[par, :, 1], st.at[par, :, 17], {"gx": (gx + 31) % 32}),
            (st.at[par, :, 16], st.at[par, :, 0], {"gx": (gx + 1) % 32}),
            (ysend.at[par, 0], hy.at[par, 1], {"gy": (gy + 3) % 4}),
            (ysend.at[par, 1], hy.at[par, 0], {"gy": (gy + 1) % 4}),
            (zsend.at[par], hz.at[par], {"row": 1 - row}),
        ]
        return [
            pltpu.make_async_remote_copy(
                src_ref=src, dst_ref=dst,
                send_sem=halo_send.at[par, i], recv_sem=halo_recv.at[par, i],
                device_id=who, device_id_type=MESH,
            )
            for i, (src, dst, who) in enumerate(plan)
        ]

    def step(number, force, meanwhile=lambda: None):
        par, nxt = number % 2, (number + 1) % 2
        last = number == STEPS - 1
        if number >= 1:
            for copy in halo_copies(nxt):
                copy.wait_send()

        def inner(x, above, below):
            laps, centers = [], []
            for f in (0, 1):
                c = st[par, f, x + 1]
                yp = jnp.where(iota_y == 31, 0.0, pltpu.roll(c, 31, 0))
                ym = jnp.where(iota_y == 0, 0.0, pltpu.roll(c, 1, 0))
                zp = jnp.where(iota_z == 127, 0.0, pltpu.roll(c, 127, 1))
                zm = jnp.where(iota_z == 0, 0.0, pltpu.roll(c, 1, 1))
                lap = -6.0 * c + yp + ym + zp + zm
                if above:
                    lap = lap + st[par, f, x + 2]
                if below:
                    lap = lap + st[par, f, x]
                laps.append(lap)
                centers.append(c)
            u, v = centers
            d = diff[x]
            product = u * v * v
            change = d * laps[0] - product + 0.04 * (1.0 - u)
            if force:
                base = (x // 8) * 256 + (x % 8) * 8
                change = change + jnp.concatenate(
                    [forced[pl.ds(pl.multiple_of(base + py * 64, 8), 8), :] for py in range(4)], axis=0
                )
            st[nxt, 0, x + 1] = u + 0.1 * change
            st[nxt, 1, x + 1] = v + 0.1 * (0.5 * d * laps[1] + product - 0.1 * v)

        def inner_body(x, carry):
            inner(x, True, True)
            return carry

        lax.fori_loop(1, 15, inner_body, 0, unroll=7)
        inner(0, True, False)
        inner(15, False, True)
        meanwhile()
        for copy in halo_copies(par)[2:]:
            copy.wait_recv()
        faces = hz[par]
        faces = jnp.where(iota_z % 2 == 0, pltpu.roll(faces, 127, 1), pltpu.roll(faces, 1, 1))
        edge_z = (iota_z == 0) | (iota_z == 127)

        def finish_plane(x, packed, above=False, below=False):
            d = 0.1 * diff[x]
            new = []
            for f in (0, 1):
                y_next = hy[par, 1, f, pl.ds(x, 1), :]
                y_prev = hy[par, 0, f, pl.ds(x, 1), :]
                halo = jnp.where(edge_z, pltpu.roll(faces, 127 - 2 * (f * 16 + x), 1), 0.0)
                halo = halo + jnp.where(iota_y == 31, y_next, jnp.where(iota_y == 0, y_prev, 0.0))
                if above:
                    halo = halo + st[par, f, x + 2]
                if below:
                    halo = halo + st[par, f, x]
                value = st[nxt, f, x + 1] + (d if f == 0 else 0.5 * d) * halo
                st[nxt, f, x + 1] = value
                new.append(value)
            if number == STEPS // 2 - 1:
                base = (x // 8) * 256 + (x % 8) * 8
                for py in range(4):
                    here = pl.ds(pl.multiple_of(base + py * 64, 8), 8)
                    tiles_u[here, :] = new[0][py * 8:py * 8 + 8, :]
                    tiles_v[here, :] = new[1][py * 8:py * 8 + 8, :]
            return packed if last else face_rows(nxt, x, new, packed)

        packed = lax.fori_loop(1, 15, finish_plane, jnp.zeros((32, 128), F32), unroll=7)
        for copy in halo_copies(par)[:2]:
            copy.wait_recv()
        packed = finish_plane(0, packed, below=True)
        packed = finish_plane(15, packed, above=True)
        if not last:
            zsend[nxt] = packed
            for copy in halo_copies(nxt):
                copy.start()

    loads[0].wait()

    def first_faces(x, packed):
        return face_rows(0, x, (st[0, 0, x + 1], st[0, 1, x + 1]), packed)

    zsend[0] = lax.fori_loop(0, 16, first_faces, jnp.zeros((32, 128), F32), unroll=4)
    pl.semaphore_wait(barrier, len(peers))
    for d in (1, 7):
        pl.semaphore_signal(near, inc=1, device_id=moved(at, "z", d), device_id_type=MESH)
    for copy in halo_copies(0):
        copy.start()

    def build_order():
        r = lax.broadcasted_iota(jnp.int32, (512, 512), 0)
        c = lax.broadcasted_iota(jnp.int32, (512, 512), 1)
        order[0] = jnp.where(c == ((r & 63) << 3) + (r >> 6), 1.0, 0.0).astype(BF16)

    def build_shares():
        r = lax.broadcasted_iota(jnp.int32, (512, 512), 0)
        c = lax.broadcasted_iota(jnp.int32, (512, 512), 1)
        for half in (0, 1):
            cell = ((r >> 7) << 7) + (((r >> 5) & 3) << 5) + half * 16
            cell = cell + (((r >> 3) & 3) << 2) + (((r >> 2) & 1) << 1) + (r & 1)
            order[1 + half] = jnp.where(c == cell, 1.0, 0.0).astype(BF16)

    loads[1].wait()
    step(0, False, build_order)
    pl.semaphore_wait(near, 2)
    for d in (2, 6):
        pl.semaphore_signal(far, inc=1, device_id=moved(at, "z", d), device_id_type=MESH)
    step(1, False, build_shares)
    pl.semaphore_wait(far, 2)
    step(2, False)

    low = lax.broadcasted_iota(jnp.int32, (16, 128), 1) < 64
    for tiles, result in ((tiles_u, inputs), (tiles_v, targets)):
        for q in range(4):
            turned[q] = tiles[q * 128:q * 128 + 128, :].T
        for m in range(4):
            for q in range(4):
                a = turned[q, pl.ds(2 * m, 16, stride=8), :]
                b = turned[q, pl.ds(2 * m + 1, 16, stride=8), :]
                even = jnp.where(low, a, pltpu.roll(b, 64, 1))
                odd = jnp.where(low, pltpu.roll(a, 64, 1), b)
                primed[q * 32:q * 32 + 16, m * 128:m * 128 + 128] = even.astype(BF16)
                primed[q * 32 + 16:q * 32 + 32, m * 128:m * 128 + 128] = odd.astype(BF16)
        result[...] = rows_of(primed[...], order[0]).astype(BF16)

    def pair_copy(i):
        if i < 3:
            src = left_in.at[1 - core] if i == 0 else left.at[i - 1, 1 - core]
            dst = left_in.at[2] if i == 0 else left.at[i - 1, 2]
        else:
            cols = pl.ds(*((0, 1024), (1024, 1024), (2048, 512))[i - 3])
            src, dst = right.at[0, :, cols], right.at[1, :, cols]
        return pltpu.make_async_remote_copy(
            src_ref=src, dst_ref=dst, send_sem=pair_send.at[i], recv_sem=pair_recv.at[i],
            device_id=mate, device_id_type=MESH,
        )

    def layer(source, weights, slopes, which):
        def body(j, carry):
            cols = pl.ds(pl.multiple_of(j * 256, 256), 256)
            value, slope = gelu_pair(rows_of(source[...], weights[:, cols]))
            slopes[:, cols] = slope
            hidden[which, :, cols] = value.astype(BF16)
            flipped = value.T.astype(BF16)
            for x in range(4):
                for half in (0, 1):
                    left[which, half, pl.ds(pl.multiple_of((j * 4 + x) * 32, 32), 32), :] = flipped[
                        x * 64 + half * 32:x * 64 + half * 32 + 32, :
                    ]
            return carry

        lax.fori_loop(0, 4, body, 0, unroll=4)

    loads[2].wait()
    layer(inputs, wf, slope1, 0)
    pair_copy(1).start()
    for half in (0, 1):
        left_in[half] = rows_of_t(order[1 + half], inputs[...]).astype(BF16)
    pair_copy(0).start()
    loads[3].wait()
    layer(hidden.at[0], wm, slope2, 1)
    pair_copy(2).start()
    loads[4].wait()
    forcing = rows_of(hidden[1], wl[...])
    right[0, :, 2048:2560] = ((forcing - targets[...].astype(F32)) * (1.0 / 128)).astype(BF16)
    pair_copy(5).start()

    def backward(error_cols, weights, slopes, first_col):
        def body(j, carry):
            cols = pl.ds(pl.multiple_of(j * 256, 256), 256)
            carried = rows_of_t(right[0, :, error_cols], weights[cols, :])
            right[0, :, pl.ds(pl.multiple_of(first_col + j * 256, 256), 256)] = (
                carried * slopes[:, cols]
            ).astype(BF16)
            return carry

        lax.fori_loop(0, 4, body, 0, unroll=4)

    def is_halved(b):
        return b // 2 in HALVED

    def halving(b):
        distance = 1 + row * 6 if b % 2 == 0 else 7 - row * 6
        return pltpu.make_async_remote_copy(
            src_ref=hgrad.at[SLOT[b], 1 - row], dst_ref=hrecv.at[SLOT[b]],
            send_sem=half_send.at[SLOT[b]], recv_sem=half_take.at[SLOT[b]],
            device_id=moved(at, "z", distance), device_id_type=MESH,
        )

    def stage(b, number, d):
        axis, k = "xy"[(b + number) % 2], SLOT[b]
        if is_halved(b):
            src, dst = (hgrad.at[k, row], hrecv1) if number == 0 else (hsum1.at[k], hrecv2)
        else:
            src, dst = (grad.at[k], recv1) if number == 0 else (sum1.at[k], recv2)
        send, take = (send1, take1) if number == 0 else (send2, take2)
        return pltpu.make_async_remote_copy(
            src_ref=src.at[(at[axis] + d) % 4], dst_ref=dst.at[k, d - 1],
            send_sem=send.at[b, d - 1], recv_sem=take.at[b, d - 1],
            device_id=moved(at, axis, d), device_id_type=MESH,
        )

    def gradient(b, own, other, cols):
        both = jnp.concatenate([own, other], axis=1)
        columns = jnp.concatenate([right[0, :, cols], right[1, :, cols]], axis=0)
        return rows_of(both, columns)

    upper_half = lax.broadcasted_iota(jnp.int32, (64, 8, 128), 1) < 4

    def keep(b, value):
        tiles = value.reshape(64, 8, 256)
        lo, hi = tiles[:, :, :128], tiles[:, :, 128:]
        even = jnp.where(upper_half, lo, pltpu.roll(hi, 4, 1))
        odd = jnp.where(upper_half, pltpu.roll(lo, 4, 1), hi)
        for zl, part in ((0, even), (1, odd)):
            part = part.reshape(4, 4, 4, 8, 128)
            for i in range(4):
                cut = part[:, i] if b % 2 == 0 else part[:, :, i]
                if is_halved(b):
                    hgrad[SLOT[b], zl, i] = cut
                else:
                    grad[SLOT[b], i, :, zl] = cut
        if is_halved(b):
            halving(b).start()
        else:
            for d in (1, 2, 3):
                stage(b, 0, d).start()

    backward(pl.ds(2048, 512), wl, slope2, 1024)
    pair_copy(4).start()
    pair_copy(2).wait_recv()
    pair_copy(5).wait_recv()
    for b in (0, 1):
        keep(b, gradient(b, left[1, core], left[1, 2], slice(2048 + b * 256, 2304 + b * 256)))
    pair_copy(1).wait_recv()
    pair_copy(4).wait_recv()
    for b in (2, 3, 4, 5):
        col = 1024 + (b - 2) * 256
        keep(b, gradient(b, left[0, core], left[0, 2], slice(col, col + 256)))
    backward(pl.ds(1024, 1024), wm, slope1, 0)
    pair_copy(3).start()
    pair_copy(0).wait_recv()
    pair_copy(3).wait_recv()
    upper = (lax.broadcasted_iota(jnp.int32, (512, 256), 0) // 2) % 2 == 0
    for b in (6, 7):
        col = (b - 6) * 256
        keep(
            b,
            jnp.where(
                upper,
                gradient(b, left_in[core], left_in[2], slice(col, col + 256)),
                gradient(b, left_in[core], left_in[2], slice(col + 512, col + 768)),
            ),
        )

    top = forcing.astype(BF16)
    rest = forcing - top.astype(F32)
    middle = rest.astype(BF16)
    rest = (rest - middle.astype(F32)).astype(BF16)
    back = rows_of_t(top, order[0]) + rows_of_t(middle, order[0]) + rows_of_t(rest, order[0])
    for m in range(4):
        for q in range(4):
            even = back[q * 32:q * 32 + 16, m * 128:m * 128 + 128]
            odd = back[q * 32 + 16:q * 32 + 32, m * 128:m * 128 + 128]
            turned[q, pl.ds(2 * m, 16, stride=8), :] = jnp.where(low, even, pltpu.roll(odd, 64, 1))
            turned[q, pl.ds(2 * m + 1, 16, stride=8), :] = jnp.where(low, pltpu.roll(even, 64, 1), odd)
    for q in range(4):
        forced[q * 128:q * 128 + 128, :] = turned[q].T
    step(3, True)

    def after_half(b):
        halving(b).wait_recv()
        hgrad[SLOT[b], row] = hgrad[SLOT[b], row] + hrecv[SLOT[b]]
        for d in (1, 2, 3):
            stage(b, 0, d).start()

    def after_first(b):
        k, me = SLOT[b], at["xy"[b % 2]]
        for d in (1, 2, 3):
            stage(b, 0, d).wait_recv()
        if is_halved(b):
            total = hgrad[k, row, me] + hrecv1[k, 0] + hrecv1[k, 1] + hrecv1[k, 2]
            for i in range(4):
                hsum1[k, i] = total[:, i]
        else:
            total = grad[k, me] + recv1[k, 0] + recv1[k, 1] + recv1[k, 2]
            for i in range(4):
                sum1[k, i] = total[:, :, i]
        for d in (1, 2, 3):
            stage(b, 1, d).start()

    def after_second(b):
        k, me = SLOT[b], at["xy"[(b + 1) % 2]]
        for d in (1, 2, 3):
            stage(b, 1, d).wait_recv()
        here = slice(b % 2 * 128, b % 2 * 128 + 128)
        if is_halved(b):
            total = hsum1[k, me] + hrecv2[k, 0] + hrecv2[k, 1] + hrecv2[k, 2]
            hpack[k // 2, :, :, here] = total
        else:
            total = sum1[k, me] + recv2[k, 0] + recv2[k, 1] + recv2[k, 2]
            pack[k // 2, :, :, here] = total.reshape(8, 8, 128)

    def stage3(piece, d):
        k = SLOT[2 * piece] // 2
        if piece in HALVED:
            src, dst = hpack.at[k, (at["z"] // 2 + d) % 4], hrecv3.at[k, d - 1]
            who = moved(at, "z", 2 * d)
        else:
            src, dst = pack.at[k, (at["z"] + d) % 8], recv3.at[k, d - 1]
            who = moved(at, "z", d)
        return pltpu.make_async_remote_copy(
            src_ref=src, dst_ref=dst,
            send_sem=send3.at[piece, d - 1], recv_sem=take3.at[piece, d - 1],
            device_id=who, device_id_type=MESH,
        )

    def hops(piece):
        return range(1, 4) if piece in HALVED else range(1, 8)

    def last_stage(piece):
        after_second(2 * piece)
        after_second(2 * piece + 1)
        for d in hops(piece):
            stage3(piece, d).start()

    def finish(piece):
        for d in hops(piece):
            stage3(piece, d).wait_recv()
        k = SLOT[2 * piece] // 2
        total = hpack[k, at["z"] // 2] if piece in HALVED else pack[k, at["z"]]
        for d in hops(piece):
            total = total + (hrecv3[k, d - 1] if piece in HALVED else recv3[k, d - 1])
        sums_out[:, piece * 256:piece * 256 + 256] = total

    after_half(2)
    after_half(3)
    after_first(0)
    after_first(1)
    after_half(4)
    after_half(5)
    after_first(6)
    after_first(7)
    step(4, True)
    after_first(2)
    after_first(3)
    last_stage(0)
    after_first(4)
    after_first(5)
    last_stage(3)
    last_stage(1)
    step(5, True)
    out = pltpu.make_async_copy(st.at[0, :, pl.ds(1, 16)], conc_out, out_sem)
    out.start()
    last_stage(2)
    for piece in (0, 3, 1, 2):
        finish(piece)

    out.wait()
    for i in range(6):
        pair_copy(i).wait_send()
    for b in range(BLOCKS):
        for d in (1, 2, 3):
            stage(b, 0, d).wait_send()
            stage(b, 1, d).wait_send()
    for piece in range(4):
        for d in hops(piece):
            stage3(piece, d).wait_send()
    for b in range(BLOCKS):
        if is_halved(b):
            halving(b).wait_send()
    for copy in halo_copies((STEPS - 1) % 2):
        copy.wait_send()


def unpack(sums, gf_out, gm_out, gl_out):
    def wide(b):
        part = sums[:, b * 128:b * 128 + 128]
        return jnp.concatenate([part[0:4], part[4:8]], axis=1)

    gl_out[...] = jnp.concatenate([wide(0), wide(1)], axis=1)
    gm_out[...] = jnp.concatenate([wide(b) for b in (2, 3, 4, 5)], axis=1)
    whole = jnp.concatenate([wide(6), wide(7)], axis=1)
    gf_out[...] = jnp.concatenate([whole[0:2], whole[2:4]], axis=1)


def per_device(concentrations, diffusivity, weight_first, weight_middle, weight_last):
    any_space = pl.BlockSpec(memory_space=pl.ANY)
    vmem = pl.BlockSpec(memory_space=pltpu.VMEM)
    dma = pltpu.SemaphoreType.DMA
    state, sums = pl.pallas_call(
        kernel,
        out_shape=(
            pltpu.VMEM((2, 16, 32, 128), F32),
            jax.ShapeDtypeStruct((8, BLOCKS * 128), F32),
        ),
        in_specs=[any_space] * 5,
        out_specs=(vmem, vmem),
        scratch_shapes=[
            pltpu.VMEM((2, 2, 18, 32, 128), F32),
            pltpu.VMEM((16, 32, 128), F32),
            pltpu.VMEM((2, 2, 2, 16, 128), F32),
            pltpu.VMEM((2, 32, 128), F32),
            pltpu.VMEM((2, 2, 2, 16, 128), F32),
            pltpu.VMEM((2, 32, 128), F32),
            pltpu.VMEM((512, 128), F32),
            pltpu.VMEM((512, 128), F32),
            pltpu.VMEM((4, 128, 128), F32),
            pltpu.VMEM((512, 128), F32),
            pltpu.VMEM((512, 1024), BF16),
            pltpu.VMEM((1024, 1024), BF16),
            pltpu.VMEM((1024, 512), BF16),
            pltpu.VMEM((3, 512, 512), BF16),
            pltpu.VMEM((128, 512), BF16),
            pltpu.VMEM((128, 512), BF16),
            pltpu.VMEM((128, 512), BF16),
            pltpu.VMEM((128, 1024), F32),
            pltpu.VMEM((128, 1024), F32),
            pltpu.VMEM((2, 128, 1024), BF16),
            pltpu.VMEM((2, 3, 512, 128), BF16),
            pltpu.VMEM((3, 512, 128), BF16),
            pltpu.VMEM((2, 128, 2560), BF16),
            pltpu.VMEM((4, 4, 4, 2, 4, 8, 128), F32),
            pltpu.VMEM((4, 3, 4, 2, 4, 8, 128), F32),
            pltpu.VMEM((4, 4, 4, 2, 8, 128), F32),
            pltpu.VMEM((4, 3, 4, 2, 8, 128), F32),
            pltpu.VMEM((2, 8, 8, 256), F32),
            pltpu.VMEM((2, 7, 8, 256), F32),
            pltpu.VMEM((4, 2, 4, 4, 4, 8, 128), F32),
            pltpu.VMEM((4, 4, 4, 4, 8, 128), F32),
            pltpu.VMEM((4, 3, 4, 4, 8, 128), F32),
            pltpu.VMEM((4, 4, 4, 8, 128), F32),
            pltpu.VMEM((4, 3, 4, 8, 128), F32),
            pltpu.VMEM((2, 4, 8, 256), F32),
            pltpu.VMEM((2, 3, 8, 256), F32),
            dma((5,)), dma, dma((2, 5)), dma((2, 5)), dma((6,)), dma((6,)),
            pltpu.SemaphoreType.REGULAR, pltpu.SemaphoreType.REGULAR,
            dma((4,)), dma((4,)),
            dma((BLOCKS, 3)), dma((BLOCKS, 3)), dma((BLOCKS, 3)), dma((BLOCKS, 3)),
            dma((4, 7)), dma((4, 7)),
        ],
        compiler_params=pltpu.CompilerParams(
            collective_id=0, has_side_effects=True, vmem_limit_bytes=56 << 20
        ),
        name="whole_step",
    )(concentrations, diffusivity, weight_first, weight_middle, weight_last)
    grads = pl.pallas_call(
        unpack,
        out_shape=(
            jax.ShapeDtypeStruct((2, 1024), F32),
            jax.ShapeDtypeStruct((4, 1024), F32),
            jax.ShapeDtypeStruct((4, 512), F32),
        ),
        in_specs=[vmem],
        out_specs=(vmem, vmem, vmem),
        name="outputs",
    )(sums)
    return (state, *grads)


def solution(mesh):
    in_specs = (P(None, "gx", "gy", "row"), P("gx", "gy", "row"), P(), P(), P())
    out_specs = (
        P(None, "gx", "gy", "row"),
        P(("gx", "gy", "row"), None),
        P(("gx", "gy", "row"), None),
        P(("gx", "gy", "row"), None),
    )
    return jax.shard_map(
        per_device, mesh=mesh, in_specs=in_specs, out_specs=out_specs, check_vma=False
    )
```

```python
import jax
import jax.numpy as jnp
from jax import lax
from jax.experimental import pallas as pl
from jax.experimental.pallas import tpu as pltpu
from jax.sharding import PartitionSpec as P

STEPS = 6
F32 = jnp.float32
BF16 = jnp.bfloat16
MESH = pl.DeviceIdType.MESH
BLOCKS = 8
HALVED = (1, 2)
SLOT = {0: 0, 1: 1, 6: 2, 7: 3, 2: 0, 3: 1, 4: 2, 5: 3}
GELU_A = 0.7978845608028654
GELU_B = 0.044715


def place():
    gx, gy, row = lax.axis_index("gx"), lax.axis_index("gy"), lax.axis_index("row")
    return {"core": gx % 2, "x": (gx // 2) % 4, "y": gy, "z": (gx // 8) * 2 + row}


def device(at):
    return {
        "gx": (at["z"] // 2) * 8 + at["x"] * 2 + at["core"],
        "gy": at["y"],
        "row": at["z"] % 2,
    }


def moved(at, axis, distance):
    size = {"core": 2, "x": 4, "y": 4, "z": 8}[axis]
    return device({**at, axis: (at[axis] + distance) % size})


def gelu_pair(values):
    squared = values * values
    bent = jnp.tanh(GELU_A * (values + GELU_B * (values * squared)))
    half = 0.5 * (1.0 + bent)
    slope = half + (0.5 * values) * (1.0 - bent * bent) * (
        GELU_A + (3.0 * GELU_A * GELU_B) * squared
    )
    return values * half, slope


def rows_of(left, right):
    return lax.dot_general(left, right, (((1,), (0,)), ((), ())), preferred_element_type=F32)


def rows_of_t(left, right):
    return lax.dot_general(left, right, (((1,), (1,)), ((), ())), preferred_element_type=F32)


def kernel(
    conc, diff_in, wf_in, wm_in, wl_in,
    conc_out, sums_out,
    st, diff, ysend, zsend, hy, hz, tiles_u, tiles_v, turned, forced,
    wf, wm, wl, order, primed, inputs, targets, slope1, slope2, hidden,
    left, left_in, right,
    grad, recv1, sum1, recv2, pack, recv3, hgrad, hrecv, hrecv1, hsum1, hrecv2, hpack, hrecv3,
    load_sem, out_sem, halo_send, halo_recv, pair_send, pair_recv,
    near, far, half_send, half_take, send1, take1, send2, take2, send3, take3,
):
    at = place()
    gx, gy, row = lax.axis_index("gx"), lax.axis_index("gy"), lax.axis_index("row")
    mate = moved(at, "core", 1)
    core = at["core"]

    loads = [
        pltpu.make_async_copy(conc, st.at[0, :, pl.ds(1, 16)], load_sem.at[0]),
        pltpu.make_async_copy(diff_in, diff, load_sem.at[1]),
        pltpu.make_async_copy(wf_in, wf, load_sem.at[2]),
        pltpu.make_async_copy(wm_in, wm, load_sem.at[3]),
        pltpu.make_async_copy(wl_in, wl, load_sem.at[4]),
    ]
    for copy in loads:
        copy.start()

    barrier = pltpu.get_barrier_semaphore()
    peers = [{"gx": (gx + 1) % 32}, {"gx": (gx + 31) % 32}]
    peers += [moved(at, "x", d) for d in (1, 2, 3)]
    peers += [moved(at, "y", d) for d in (1, 2, 3)]
    peers += [moved(at, "z", d) for d in (1, 7)]
    for peer in peers:
        pl.semaphore_signal(barrier, inc=1, device_id=peer, device_id_type=MESH)

    iota_y = lax.broadcasted_iota(jnp.int32, (32, 128), 0)
    iota_z = lax.broadcasted_iota(jnp.int32, (32, 128), 1)
    pair_z = iota_z // 2

    def face_rows(par, x, new, packed):
        for f in (0, 1):
            ysend[par, 0, f, pl.ds(x, 1), :] = new[f][0:1, :]
            ysend[par, 1, f, pl.ds(x, 1), :] = new[f][31:32, :]
            k = f * 16 + x
            packed = jnp.where(pair_z == k, pltpu.roll(new[f], 2 * k + 1, 1), packed)
        return packed

    def halo_copies(par):
        plan = [
            (st.at[par, :, 1], st.at[par, :, 17], {"gx": (gx + 31) % 32}),
            (st.at[par, :, 16], st.at[par, :, 0], {"gx": (gx + 1) % 32}),
            (ysend.at[par, 0], hy.at[par, 1], {"gy": (gy + 3) % 4}),
            (ysend.at[par, 1], hy.at[par, 0], {"gy": (gy + 1) % 4}),
            (zsend.at[par], hz.at[par], {"row": 1 - row}),
        ]
        return [
            pltpu.make_async_remote_copy(
                src_ref=src, dst_ref=dst,
                send_sem=halo_send.at[par, i], recv_sem=halo_recv.at[par, i],
                device_id=who, device_id_type=MESH,
            )
            for i, (src, dst, who) in enumerate(plan)
        ]

    def step(number, force, meanwhile=lambda: None):
        par, nxt = number % 2, (number + 1) % 2
        last = number == STEPS - 1
        if number >= 1:
            for copy in halo_copies(nxt):
                copy.wait_send()

        def inner(x, above, below):
            laps, centers = [], []
            for f in (0, 1):
                c = st[par, f, x + 1]
                yp = jnp.where(iota_y == 31, 0.0, pltpu.roll(c, 31, 0))
                ym = jnp.where(iota_y == 0, 0.0, pltpu.roll(c, 1, 0))
                zp = jnp.where(iota_z == 127, 0.0, pltpu.roll(c, 127, 1))
                zm = jnp.where(iota_z == 0, 0.0, pltpu.roll(c, 1, 1))
                lap = -6.0 * c + yp + ym + zp + zm
                if above:
                    lap = lap + st[par, f, x + 2]
                if below:
                    lap = lap + st[par, f, x]
                laps.append(lap)
                centers.append(c)
            u, v = centers
            d = diff[x]
            product = u * v * v
            change = d * laps[0] - product + 0.04 * (1.0 - u)
            if force:
                base = (x // 8) * 256 + (x % 8) * 8
                change = change + jnp.concatenate(
                    [forced[pl.ds(pl.multiple_of(base + py * 64, 8), 8), :] for py in range(4)], axis=0
                )
            st[nxt, 0, x + 1] = u + 0.1 * change
            st[nxt, 1, x + 1] = v + 0.1 * (0.5 * d * laps[1] + product - 0.1 * v)

        def inner_body(x, carry):
            inner(x, True, True)
            return carry

        lax.fori_loop(1, 15, inner_body, 0, unroll=7)
        inner(0, True, False)
        inner(15, False, True)
        meanwhile()
        for copy in halo_copies(par)[2:]:
            copy.wait_recv()
        faces = hz[par]
        faces = jnp.where(iota_z % 2 == 0, pltpu.roll(faces, 127, 1), pltpu.roll(faces, 1, 1))
        edge_z = (iota_z == 0) | (iota_z == 127)

        def finish_plane(x, packed, above=False, below=False):
            d = 0.1 * diff[x]
            new = []
            for f in (0, 1):
                y_next = hy[par, 1, f, pl.ds(x, 1), :]
                y_prev = hy[par, 0, f, pl.ds(x, 1), :]
                halo = jnp.where(edge_z, pltpu.roll(faces, 127 - 2 * (f * 16 + x), 1), 0.0)
                halo = halo + jnp.where(iota_y == 31, y_next, jnp.where(iota_y == 0, y_prev, 0.0))
                if above:
                    halo = halo + st[par, f, x + 2]
                if below:
                    halo = halo + st[par, f, x]
                value = st[nxt, f, x + 1] + (d if f == 0 else 0.5 * d) * halo
                st[nxt, f, x + 1] = value
                new.append(value)
            if number == STEPS // 2 - 1:
                base = (x // 8) * 256 + (x % 8) * 8
                for py in range(4):
                    here = pl.ds(pl.multiple_of(base + py * 64, 8), 8)
                    tiles_u[here, :] = new[0][py * 8:py * 8 + 8, :]
                    tiles_v[here, :] = new[1][py * 8:py * 8 + 8, :]
            return packed if last else face_rows(nxt, x, new, packed)

        packed = lax.fori_loop(1, 15, finish_plane, jnp.zeros((32, 128), F32), unroll=7)
        for copy in halo_copies(par)[:2]:
            copy.wait_recv()
        packed = finish_plane(0, packed, below=True)
        packed = finish_plane(15, packed, above=True)
        if not last:
            zsend[nxt] = packed
            for copy in halo_copies(nxt):
                copy.start()

    loads[0].wait()

    def first_faces(x, packed):
        return face_rows(0, x, (st[0, 0, x + 1], st[0, 1, x + 1]), packed)

    zsend[0] = lax.fori_loop(0, 16, first_faces, jnp.zeros((32, 128), F32), unroll=4)
    pl.semaphore_wait(barrier, len(peers))
    for d in (1, 7):
        pl.semaphore_signal(near, inc=1, device_id=moved(at, "z", d), device_id_type=MESH)
    for copy in halo_copies(0):
        copy.start()

    def build_order():
        r = lax.broadcasted_iota(jnp.int32, (512, 512), 0)
        c = lax.broadcasted_iota(jnp.int32, (512, 512), 1)
        order[0] = jnp.where(c == ((r & 63) << 3) + (r >> 6), 1.0, 0.0).astype(BF16)

    def build_shares():
        r = lax.broadcasted_iota(jnp.int32, (512, 512), 0)
        c = lax.broadcasted_iota(jnp.int32, (512, 512), 1)
        for half in (0, 1):
            cell = ((r >> 7) << 7) + (((r >> 5) & 3) << 5) + half * 16
            cell = cell + (((r >> 3) & 3) << 2) + (((r >> 2) & 1) << 1) + (r & 1)
            order[1 + half] = jnp.where(c == cell, 1.0, 0.0).astype(BF16)

    loads[1].wait()
    step(0, False, build_order)
    pl.semaphore_wait(near, 2)
    for d in (2, 6):
        pl.semaphore_signal(far, inc=1, device_id=moved(at, "z", d), device_id_type=MESH)
    step(1, False, build_shares)
    pl.semaphore_wait(far, 2)
    step(2, False)

    low = lax.broadcasted_iota(jnp.int32, (16, 128), 1) < 64
    for tiles, result in ((tiles_u, inputs), (tiles_v, targets)):
        for q in range(4):
            turned[q] = tiles[q * 128:q * 128 + 128, :].T
        for m in range(4):
            for q in range(4):
                a = turned[q, pl.ds(2 * m, 16, stride=8), :]
                b = turned[q, pl.ds(2 * m + 1, 16, stride=8), :]
                even = jnp.where(low, a, pltpu.roll(b, 64, 1))
                odd = jnp.where(low, pltpu.roll(a, 64, 1), b)
                primed[q * 32:q * 32 + 16, m * 128:m * 128 + 128] = even.astype(BF16)
                primed[q * 32 + 16:q * 32 + 32, m * 128:m * 128 + 128] = odd.astype(BF16)
        result[...] = rows_of(primed[...], order[0]).astype(BF16)

    def pair_copy(i):
        if i < 3:
            src = left_in.at[1 - core] if i == 0 else left.at[i - 1, 1 - core]
            dst = left_in.at[2] if i == 0 else left.at[i - 1, 2]
        else:
            cols = pl.ds(*((0, 1024), (1024, 1024), (2048, 512))[i - 3])
            src, dst = right.at[0, :, cols], right.at[1, :, cols]
        return pltpu.make_async_remote_copy(
            src_ref=src, dst_ref=dst, send_sem=pair_send.at[i], recv_sem=pair_recv.at[i],
            device_id=mate, device_id_type=MESH,
        )

    def layer(source, weights, slopes, which):
        def body(j, carry):
            cols = pl.ds(pl.multiple_of(j * 256, 256), 256)
            value, slope = gelu_pair(rows_of(source[...], weights[:, cols]))
            slopes[:, cols] = slope
            hidden[which, :, cols] = value.astype(BF16)
            flipped = value.T.astype(BF16)
            for x in range(4):
                for half in (0, 1):
                    left[which, half, pl.ds(pl.multiple_of((j * 4 + x) * 32, 32), 32), :] = flipped[
                        x * 64 + half * 32:x * 64 + half * 32 + 32, :
                    ]
            return carry

        lax.fori_loop(0, 4, body, 0, unroll=4)

    loads[2].wait()
    layer(inputs, wf, slope1, 0)
    pair_copy(1).start()
    for half in (0, 1):
        left_in[half] = rows_of_t(order[1 + half], inputs[...]).astype(BF16)
    pair_copy(0).start()
    loads[3].wait()
    layer(hidden.at[0], wm, slope2, 1)
    pair_copy(2).start()
    loads[4].wait()
    forcing = rows_of(hidden[1], wl[...])
    right[0, :, 2048:2560] = ((forcing - targets[...].astype(F32)) * (1.0 / 128)).astype(BF16)
    pair_copy(5).start()

    def backward(error_cols, weights, slopes, first_col):
        def body(j, carry):
            cols = pl.ds(pl.multiple_of(j * 256, 256), 256)
            carried = rows_of_t(right[0, :, error_cols], weights[cols, :])
            right[0, :, pl.ds(pl.multiple_of(first_col + j * 256, 256), 256)] = (
                carried * slopes[:, cols]
            ).astype(BF16)
            return carry

        lax.fori_loop(0, 4, body, 0, unroll=4)

    def is_halved(b):
        return b // 2 in HALVED

    def halving(b):
        distance = 1 + row * 6 if b % 2 == 0 else 7 - row * 6
        return pltpu.make_async_remote_copy(
            src_ref=hgrad.at[SLOT[b], 1 - row], dst_ref=hrecv.at[SLOT[b]],
            send_sem=half_send.at[SLOT[b]], recv_sem=half_take.at[SLOT[b]],
            device_id=moved(at, "z", distance), device_id_type=MESH,
        )

    def stage(b, number, d):
        axis, k = "xy"[(b + number) % 2], SLOT[b]
        if is_halved(b):
            src, dst = (hgrad.at[k, row], hrecv1) if number == 0 else (hsum1.at[k], hrecv2)
        else:
            src, dst = (grad.at[k], recv1) if number == 0 else (sum1.at[k], recv2)
        send, take = (send1, take1) if number == 0 else (send2, take2)
        return pltpu.make_async_remote_copy(
            src_ref=src.at[(at[axis] + d) % 4], dst_ref=dst.at[k, d - 1],
            send_sem=send.at[b, d - 1], recv_sem=take.at[b, d - 1],
            device_id=moved(at, axis, d), device_id_type=MESH,
        )

    def gradient(b, own, other, cols):
        both = jnp.concatenate([own, other], axis=1)
        columns = jnp.concatenate([right[0, :, cols], right[1, :, cols]], axis=0)
        return rows_of(both, columns)

    upper_half = lax.broadcasted_iota(jnp.int32, (64, 8, 128), 1) < 4

    def keep(b, value):
        tiles = value.reshape(64, 8, 256)
        lo, hi = tiles[:, :, :128], tiles[:, :, 128:]
        even = jnp.where(upper_half, lo, pltpu.roll(hi, 4, 1))
        odd = jnp.where(upper_half, pltpu.roll(lo, 4, 1), hi)
        for zl, part in ((0, even), (1, odd)):
            part = part.reshape(4, 4, 4, 8, 128)
            for i in range(4):
                cut = part[:, i] if b % 2 == 0 else part[:, :, i]
                if is_halved(b):
                    hgrad[SLOT[b], zl, i] = cut
                else:
                    grad[SLOT[b], i, :, zl] = cut
        if is_halved(b):
            halving(b).start()
        else:
            for d in (2, 1, 3):
                stage(b, 0, d).start()

    backward(pl.ds(2048, 512), wl, slope2, 1024)
    pair_copy(4).start()
    pair_copy(2).wait_recv()
    pair_copy(5).wait_recv()
    for b in (0, 1):
        keep(b, gradient(b, left[1, core], left[1, 2], slice(2048 + b * 256, 2304 + b * 256)))
    pair_copy(1).wait_recv()
    pair_copy(4).wait_recv()
    for b in (2, 3, 4, 5):
        col = 1024 + (b - 2) * 256
        keep(b, gradient(b, left[0, core], left[0, 2], slice(col, col + 256)))
    backward(pl.ds(1024, 1024), wm, slope1, 0)
    pair_copy(3).start()
    pair_copy(0).wait_recv()
    pair_copy(3).wait_recv()
    upper = (lax.broadcasted_iota(jnp.int32, (512, 256), 0) // 2) % 2 == 0
    for b in (6, 7):
        col = (b - 6) * 256
        keep(
            b,
            jnp.where(
                upper,
                gradient(b, left_in[core], left_in[2], slice(col, col + 256)),
                gradient(b, left_in[core], left_in[2], slice(col + 512, col + 768)),
            ),
        )

    top = forcing.astype(BF16)
    rest = forcing - top.astype(F32)
    middle = rest.astype(BF16)
    rest = (rest - middle.astype(F32)).astype(BF16)
    back = rows_of_t(top, order[0]) + rows_of_t(middle, order[0]) + rows_of_t(rest, order[0])
    for m in range(4):
        for q in range(4):
            even = back[q * 32:q * 32 + 16, m * 128:m * 128 + 128]
            odd = back[q * 32 + 16:q * 32 + 32, m * 128:m * 128 + 128]
            turned[q, pl.ds(2 * m, 16, stride=8), :] = jnp.where(low, even, pltpu.roll(odd, 64, 1))
            turned[q, pl.ds(2 * m + 1, 16, stride=8), :] = jnp.where(low, pltpu.roll(even, 64, 1), odd)
    for q in range(4):
        forced[q * 128:q * 128 + 128, :] = turned[q].T
    step(3, True)

    def after_half(b):
        halving(b).wait_recv()
        hgrad[SLOT[b], row] = hgrad[SLOT[b], row] + hrecv[SLOT[b]]
        for d in (2, 1, 3):
            stage(b, 0, d).start()

    def after_first(b):
        k, me = SLOT[b], at["xy"[b % 2]]
        for d in (1, 2, 3):
            stage(b, 0, d).wait_recv()
        if is_halved(b):
            total = hgrad[k, row, me] + hrecv1[k, 0] + hrecv1[k, 1] + hrecv1[k, 2]
            for i in range(4):
                hsum1[k, i] = total[:, i]
        else:
            total = grad[k, me] + recv1[k, 0] + recv1[k, 1] + recv1[k, 2]
            for i in range(4):
                sum1[k, i] = total[:, :, i]
        for d in (2, 1, 3):
            stage(b, 1, d).start()

    def after_second(b):
        k, me = SLOT[b], at["xy"[(b + 1) % 2]]
        for d in (1, 2, 3):
            stage(b, 1, d).wait_recv()
        here = slice(b % 2 * 128, b % 2 * 128 + 128)
        if is_halved(b):
            total = hsum1[k, me] + hrecv2[k, 0] + hrecv2[k, 1] + hrecv2[k, 2]
            hpack[k // 2, :, :, here] = total
        else:
            total = sum1[k, me] + recv2[k, 0] + recv2[k, 1] + recv2[k, 2]
            pack[k // 2, :, :, here] = total.reshape(8, 8, 128)

    def stage3(piece, d):
        k = SLOT[2 * piece] // 2
        if piece in HALVED:
            src, dst = hpack.at[k, (at["z"] // 2 + d) % 4], hrecv3.at[k, d - 1]
            who = moved(at, "z", 2 * d)
        else:
            src, dst = pack.at[k, (at["z"] + d) % 8], recv3.at[k, d - 1]
            who = moved(at, "z", d)
        return pltpu.make_async_remote_copy(
            src_ref=src, dst_ref=dst,
            send_sem=send3.at[piece, d - 1], recv_sem=take3.at[piece, d - 1],
            device_id=who, device_id_type=MESH,
        )

    def hops(piece):
        return range(1, 4) if piece in HALVED else range(1, 8)

    def last_stage(piece):
        after_second(2 * piece)
        after_second(2 * piece + 1)
        for d in sorted(hops(piece), key=lambda d: -min(d, len(hops(piece)) + 1 - d)):
            stage3(piece, d).start()

    def finish(piece):
        for d in hops(piece):
            stage3(piece, d).wait_recv()
        k = SLOT[2 * piece] // 2
        total = hpack[k, at["z"] // 2] if piece in HALVED else pack[k, at["z"]]
        for d in hops(piece):
            total = total + (hrecv3[k, d - 1] if piece in HALVED else recv3[k, d - 1])
        sums_out[:, piece * 256:piece * 256 + 256] = total

    after_half(2)
    after_half(3)
    after_first(0)
    after_first(1)
    after_half(4)
    after_half(5)
    after_first(6)
    after_first(7)
    step(4, True)
    after_first(2)
    after_first(3)
    last_stage(0)
    after_first(4)
    after_first(5)
    last_stage(3)
    last_stage(1)
    last_stage(2)
    step(5, True)
    out = pltpu.make_async_copy(st.at[0, :, pl.ds(1, 16)], conc_out, out_sem)
    out.start()
    for piece in (0, 3, 1, 2):
        finish(piece)

    out.wait()
    for i in range(6):
        pair_copy(i).wait_send()
    for b in range(BLOCKS):
        for d in (1, 2, 3):
            stage(b, 0, d).wait_send()
            stage(b, 1, d).wait_send()
    for piece in range(4):
        for d in hops(piece):
            stage3(piece, d).wait_send()
    for b in range(BLOCKS):
        if is_halved(b):
            halving(b).wait_send()
    for copy in halo_copies((STEPS - 1) % 2):
        copy.wait_send()


def unpack(sums, gf_out, gm_out, gl_out):
    def wide(b):
        part = sums[:, b * 128:b * 128 + 128]
        return jnp.concatenate([part[0:4], part[4:8]], axis=1)

    gl_out[...] = jnp.concatenate([wide(0), wide(1)], axis=1)
    gm_out[...] = jnp.concatenate([wide(b) for b in (2, 3, 4, 5)], axis=1)
    whole = jnp.concatenate([wide(6), wide(7)], axis=1)
    gf_out[...] = jnp.concatenate([whole[0:2], whole[2:4]], axis=1)


def per_device(concentrations, diffusivity, weight_first, weight_middle, weight_last):
    any_space = pl.BlockSpec(memory_space=pl.ANY)
    vmem = pl.BlockSpec(memory_space=pltpu.VMEM)
    dma = pltpu.SemaphoreType.DMA
    state, sums = pl.pallas_call(
        kernel,
        out_shape=(
            pltpu.VMEM((2, 16, 32, 128), F32),
            jax.ShapeDtypeStruct((8, BLOCKS * 128), F32),
        ),
        in_specs=[any_space] * 5,
        out_specs=(vmem, vmem),
        scratch_shapes=[
            pltpu.VMEM((2, 2, 18, 32, 128), F32),
            pltpu.VMEM((16, 32, 128), F32),
            pltpu.VMEM((2, 2, 2, 16, 128), F32),
            pltpu.VMEM((2, 32, 128), F32),
            pltpu.VMEM((2, 2, 2, 16, 128), F32),
            pltpu.VMEM((2, 32, 128), F32),
            pltpu.VMEM((512, 128), F32),
            pltpu.VMEM((512, 128), F32),
            pltpu.VMEM((4, 128, 128), F32),
            pltpu.VMEM((512, 128), F32),
            pltpu.VMEM((512, 1024), BF16),
            pltpu.VMEM((1024, 1024), BF16),
            pltpu.VMEM((1024, 512), BF16),
            pltpu.VMEM((3, 512, 512), BF16),
            pltpu.VMEM((128, 512), BF16),
            pltpu.VMEM((128, 512), BF16),
            pltpu.VMEM((128, 512), BF16),
            pltpu.VMEM((128, 1024), F32),
            pltpu.VMEM((128, 1024), F32),
            pltpu.VMEM((2, 128, 1024), BF16),
            pltpu.VMEM((2, 3, 512, 128), BF16),
            pltpu.VMEM((3, 512, 128), BF16),
            pltpu.VMEM((2, 128, 2560), BF16),
            pltpu.VMEM((4, 4, 4, 2, 4, 8, 128), F32),
            pltpu.VMEM((4, 3, 4, 2, 4, 8, 128), F32),
            pltpu.VMEM((4, 4, 4, 2, 8, 128), F32),
            pltpu.VMEM((4, 3, 4, 2, 8, 128), F32),
            pltpu.VMEM((2, 8, 8, 256), F32),
            pltpu.VMEM((2, 7, 8, 256), F32),
            pltpu.VMEM((4, 2, 4, 4, 4, 8, 128), F32),
            pltpu.VMEM((4, 4, 4, 4, 8, 128), F32),
            pltpu.VMEM((4, 3, 4, 4, 8, 128), F32),
            pltpu.VMEM((4, 4, 4, 8, 128), F32),
            pltpu.VMEM((4, 3, 4, 8, 128), F32),
            pltpu.VMEM((2, 4, 8, 256), F32),
            pltpu.VMEM((2, 3, 8, 256), F32),
            dma((5,)), dma, dma((2, 5)), dma((2, 5)), dma((6,)), dma((6,)),
            pltpu.SemaphoreType.REGULAR, pltpu.SemaphoreType.REGULAR,
            dma((4,)), dma((4,)),
            dma((BLOCKS, 3)), dma((BLOCKS, 3)), dma((BLOCKS, 3)), dma((BLOCKS, 3)),
            dma((4, 7)), dma((4, 7)),
        ],
        compiler_params=pltpu.CompilerParams(
            collective_id=0, has_side_effects=True, vmem_limit_bytes=56 << 20
        ),
        name="whole_step",
    )(concentrations, diffusivity, weight_first, weight_middle, weight_last)
    grads = pl.pallas_call(
        unpack,
        out_shape=(
            jax.ShapeDtypeStruct((2, 1024), F32),
            jax.ShapeDtypeStruct((4, 1024), F32),
            jax.ShapeDtypeStruct((4, 512), F32),
        ),
        in_specs=[vmem],
        out_specs=(vmem, vmem, vmem),
        name="outputs",
    )(sums)
    return (state, *grads)


def solution(mesh):
    in_specs = (P(None, "gx", "gy", "row"), P("gx", "gy", "row"), P(), P(), P())
    out_specs = (
        P(None, "gx", "gy", "row"),
        P(("gx", "gy", "row"), None),
        P(("gx", "gy", "row"), None),
        P(("gx", "gy", "row"), None),
    )
    return jax.shard_map(
        per_device, mesh=mesh, in_specs=in_specs, out_specs=out_specs, check_vma=False
    )
```
